128 devices in a mesh: shot: 16 (over z, x), sub: 8 (over y, core).
Axes of the slice: x: 4, y: 4, z: 4, core: 2. Of those that a mesh axis runs over, the one named last changes fastest.
Arguments:
- stiffness: float32 [128, 32, 384], P('sub'), may hold values from 0.04 to 0.15
- buoyancy_first: float32 [128, 32, 384], P('sub'), may hold values from 0.6 to 1.3
- buoyancy_second: float32 [128, 32, 384], P('sub'), may hold values from 0.6 to 1.3
- buoyancy_third: float32 [128, 32, 384], P('sub'), may hold values from 0.6 to 1.3
- adjoint_before: float32 [16, 128, 32, 384], P('shot', 'sub'), may hold values from -6 to 6
- adjoint_current: float32 [16, 128, 32, 384], P('shot', 'sub'), may hold values from -6 to 6
- forward_field: bfloat16 [16, 8, 128, 32, 384], P('shot', None, 'sub'), may hold values from -6 to 6
- traces: float32 [65536, 256], P(('shot', 'sub')), may hold values from -6 to 6
- receiver_target: int32 [65536, 1], P(('shot', 'sub')), may hold values from 0 to 127; in each aligned block of 512 rows (0 to 511, 512 to 1023, ...) at most 6 rows name the same one
- receiver_cell: int32 [65536], P(('shot', 'sub')), may hold values from 0 to 196607
- source_cell: int32 [16, 3], P('shot'), may hold values from 0 to 31
Outputs:
- gradient: float32 [128, 12288], P('sub', 'shot')
- adjoint_earlier: float32 [16, 128, 32, 384], P('shot', 'sub')
- adjoint_latest: float32 [16, 128, 32, 384], P('shot', 'sub')
The draws below stay inside these ranges and needn't reach their ends.
Inputs may be any that keep to these rules, and one draw needn't show every extreme that they name: `receiver_target`: at most 6 of the receivers stored on one device share a value, and 6 is reached. `receiver_cell`: flattened with the first dimension slowest.
All inputs are finite; a program needn't handle non-finite values.
Results may differ from the reference program's by a relative error of at most 0.0003.
Values sent between devices are 32-bit elements; how exact they have to be, the bound alone decides.
No kernel may reach another device: no remote copies, remote signals or barrier semaphores. Data moves between devices by JAX's collectives and lax.ppermute only.
A program may use at most 128 MiB of HBM per device.

```python
import math
import jax
import jax.numpy as jnp
import numpy as np
from jax import lax

CX = 16
NY = 32
NZ = 384
STEPS = 8
SAMPLES = 256
R_DEV = 512
MUTE = 6
NX = 128
CELLS = 196608
GROUPS = 16
R_ALL = 65536
CAP = 6
N_SHOT = 16
N_SUB = 8
DEVICES = 128


def set_ends(entries, key, least, high):
    longest = entries.shape.index(max(entries.shape))
    spots = []
    for shift in (0, 1):
        where = [jax.random.randint(jax.random.fold_in(key, axis), (), 0, length) for axis, length in enumerate(entries.shape)]
        where[longest] = (where[longest] + shift) % entries.shape[longest]
        spots.append(tuple(where))
    return entries.at[spots[0]].set(least).at[spots[1]].set(high)


def shard_levels(rng, shape, shards, least, top_value):
    def one(dim, blocks):
        draws = jax.random.uniform(jax.random.fold_in(jax.random.fold_in(rng, 6), dim), (blocks,), jnp.float32, least / len(shards), top_value / len(shards))
        return jnp.repeat(jnp.exp(draws), shape[dim] // blocks).reshape((-1,) + (1,) * (len(shape) - dim - 1))

    factor_of = one(*shards[0])
    for cut in shards[1:]:
        factor_of = factor_of * one(*cut)
    return factor_of


def assign_block(stream_key, own, number, rows, number_of, top, bound, lean):
    sequence = jax.random.permutation(stream_key, number_of)
    crowded, ordinary = shares(number_of, rows * top, bound, lean, True), shares(number_of, rows * top, bound, lean, False)
    places = jnp.arange(number_of)

    def named(tallies, rotation):
        used = int((tallies > 0).sum())
        fixed = max(1, used // 4)
        moved = fixed + (places - fixed + rotation * (used - fixed)) % max(1, number_of - fixed)
        return jnp.zeros((number_of,), jnp.int32).at[sequence[jnp.where(places < fixed, places, moved)]].set(jnp.asarray(tallies, jnp.int32))

    tallies = jnp.where(number % 4 == 0, named(crowded, number // 4), named(ordinary, number - number // 4 - 1))
    mixed = jax.random.permutation(jax.random.fold_in(own, 3), number_of)
    source_of, sink = mixed[0:number_of // 2 * 2:2], mixed[1:number_of // 2 * 2:2]
    margin = jnp.minimum(tallies[source_of] - 1, bound - tallies[sink]) // 2
    margin = jnp.where((source_of == sequence[0]) | (sink == sequence[0]) | (tallies[sink] == 0), 0, jnp.maximum(margin, 0))
    moved = jax.random.randint(jax.random.fold_in(own, 4), (number_of // 2,), 0, 1 << 20) % (margin + 1)
    tallies = tallies.at[source_of].add(-moved).at[sink].add(moved)
    labels = jnp.searchsorted(jnp.cumsum(tallies), jnp.arange(rows * top), side="right").astype(jnp.int32)
    grid = labels.reshape(top, rows).T
    grid = grid[jax.random.permutation(jax.random.fold_in(own, 1), rows)]
    rotation = jax.random.randint(jax.random.fold_in(own, 2), (rows, 1), 0, top)
    return jnp.take_along_axis(grid, (jnp.arange(top)[None, :] + rotation) % top, axis=1)


def shares(count, total, limit, slope, full):
    portions = [(1 << 20) // math.isqrt(standing ** slope) + 1 for standing in range(1, count + 1)]
    largest = limit if full else min(limit, max(-(-total // count), total * portions[0] // sum(portions)))
    least = 1 if total - largest >= count - 1 else 0
    given, surplus = [largest] + [least] * (count - 1), total - largest - least * (count - 1)
    while surplus > 0:
        movable = [i for i in range(1, count) if given[i] < largest] or [i for i in range(1, count) if given[i] < limit]
        pool, remaining = sum([portions[i] for i in movable]), surplus
        for i in movable:
            more = min(limit - given[i], max(1, remaining * portions[i] // pool), surplus)
            given[i] = given[i] + more
            surplus = surplus - more
    return np.array(given)


def normal_values(own_key, shape, spread, reach, pieces=(), held_as=jnp.bfloat16):
    gain = shard_levels(own_key, shape, pieces, -0.22, 0.18) if pieces else 1.0
    drawn = jax.random.normal(own_key, shape, jnp.float32) * spread * gain
    return jnp.minimum(jnp.maximum(drawn, -reach), reach).astype(held_as)


def setup_inputs(seed: int = 0) -> dict:
    keys = jax.random.split(jax.random.key(seed), 12)
    stiffness = jnp.clip(jnp.exp(math.log(0.15) - 1.3217559 * jax.random.uniform(keys[0], (NX, NY, NZ), jnp.float32) ** shard_levels(keys[0], (NX, NY, NZ), ((0, 8),), -0.2, 0.2)), 0.04, 0.15)
    buoyancy_first = jnp.clip(jnp.exp(math.log(1.3) - 0.7731898 * jax.random.uniform(keys[1], (NX, NY, NZ), jnp.float32) ** shard_levels(keys[1], (NX, NY, NZ), ((0, 8),), -0.2, 0.2)), 0.6, 1.3)
    buoyancy_second = jnp.clip(jnp.exp(math.log(1.3) - 0.7731898 * jax.random.uniform(keys[2], (NX, NY, NZ), jnp.float32) ** shard_levels(keys[2], (NX, NY, NZ), ((0, 8),), -0.2, 0.2)), 0.6, 1.3)
    buoyancy_third = jnp.clip(jnp.exp(math.log(1.3) - 0.7731898 * jax.random.uniform(keys[3], (NX, NY, NZ), jnp.float32) ** shard_levels(keys[3], (NX, NY, NZ), ((0, 8),), -0.2, 0.2)), 0.6, 1.3)
    adjoint_before = normal_values(keys[4], (GROUPS, NX, NY, NZ), 1.0, 6.0, ((0, 16), (1, 8)), jnp.float32)
    adjoint_current = normal_values(keys[5], (GROUPS, NX, NY, NZ), 1.0, 6.0, ((0, 16), (1, 8)), jnp.float32)
    forward_field = normal_values(keys[6], (GROUPS, STEPS, NX, NY, NZ), 1.0, 6.0, ((0, 16), (2, 8)))
    traces = normal_values(keys[7], (R_ALL, SAMPLES), 1.0, 6.0, ((0, 128),), jnp.float32)
    receiver_target_keys = jax.random.split(jax.random.fold_in(keys[8], 1), R_ALL // R_DEV)
    receiver_target_turns = jax.random.permutation(jax.random.fold_in(keys[8], 3), R_ALL // R_DEV)
    receiver_target = jax.vmap(lambda own, number: assign_block(jax.random.fold_in(keys[8], 2), own, number, R_DEV, DEVICES, 1, CAP, 2))(receiver_target_keys, receiver_target_turns).reshape((R_ALL, 1))
    receiver_cell = set_ends(jax.random.randint(keys[9], (R_ALL,), 0, CELLS), jax.random.fold_in(keys[9], 1), 0, CELLS - 1).astype(jnp.int32)
    source_cell = set_ends(jax.random.randint(keys[10], (GROUPS, 3), 0, min(NX, min(NY, NZ))), jax.random.fold_in(keys[10], 1), 0, (min(NX, min(NY, NZ))) - 1).astype(jnp.int32)
    return dict(stiffness=stiffness, buoyancy_first=buoyancy_first, buoyancy_second=buoyancy_second, buoyancy_third=buoyancy_third, adjoint_before=adjoint_before, adjoint_current=adjoint_current, forward_field=forward_field, traces=traces, receiver_target=receiver_target, receiver_cell=receiver_cell, source_cell=source_cell)


COEFFS = (1225.0 / 1024.0, -245.0 / 3072.0, 49.0 / 5120.0, -5.0 / 7168.0)
DAMP = 0.1


def take_slice(extended, dimension, offset, length):
    return lax.slice_in_dim(extended, offset, offset + length, axis=dimension)


def forward_difference(extended, dimension, offset, length):
    summed = COEFFS[0] * (take_slice(extended, dimension, offset + 1, length) - take_slice(extended, dimension, offset, length))
    for order in range(2, 5):
        summed = summed + COEFFS[order - 1] * (take_slice(extended, dimension, offset + order, length) - take_slice(extended, dimension, offset + 1 - order, length))
    return summed


def backward_difference(extended, dimension, offset, length):
    summed = COEFFS[0] * (take_slice(extended, dimension, offset, length) - take_slice(extended, dimension, offset - 1, length))
    for order in range(2, 5):
        summed = summed + COEFFS[order - 1] * (take_slice(extended, dimension, offset + order - 1, length) - take_slice(extended, dimension, offset - order, length))
    return summed


def pad_along(wave_field, dimension, amount):
    widths = [(0, 0)] * wave_field.ndim
    widths[dimension] = (amount, amount)
    return jnp.pad(wave_field, widths)


def local_divergence(wave_field, buoyancy, dimension):
    length = wave_field.shape[dimension]
    flux_field = buoyancy * forward_difference(pad_along(wave_field, dimension, 4), dimension, 4, length)
    return backward_difference(pad_along(flux_field, dimension, 4), dimension, 4, length)


def trace_kernel(sample_count, step_count):
    sample_pos = jnp.arange(sample_count, dtype=jnp.float32)[:, None]
    centers = (jnp.arange(step_count, dtype=jnp.float32)[None, :] + 0.5) * (sample_count / step_count)
    return 0.25 * jnp.exp(-jnp.abs(sample_pos - centers) / (sample_count / 8.0))


def reference(stiffness, buoyancy_first, buoyancy_second, buoyancy_third, adjoint_before, adjoint_current, forward_field, traces, receiver_target, receiver_cell, source_cell):
    kernel = trace_kernel(SAMPLES, STEPS)
    values = jnp.dot(traces, kernel, precision=lax.Precision.HIGHEST, preferred_element_type=jnp.float32)
    target = receiver_target[:, 0]
    group_of = target // N_SUB
    flat_cell = ((target % N_SUB) * (CX * NY * NZ) + receiver_cell).astype(jnp.int32)
    total_cells = NX * NY * NZ
    coord_first = jnp.arange(NX, dtype=jnp.float32)[:, None, None]
    coord_second = jnp.arange(NY, dtype=jnp.float32)[None, :, None]
    coord_third = jnp.arange(NZ, dtype=jnp.float32)[None, None, :]

    def one_group(carry, packed):
        summed_image, summed_light = carry
        group_id, earlier, current, forward_now, source_at = packed
        belongs = group_of == group_id
        chosen = jnp.where(belongs[:, None], values, jnp.float32(0.0))
        injection = jnp.zeros((STEPS, total_cells), jnp.float32).at[:, flat_cell].add(chosen.T)
        image_sum = jnp.zeros((NX, NY, NZ), jnp.float32)
        illumination = jnp.zeros((NX, NY, NZ), jnp.float32)
        for moment in range(STEPS):
            divergence = local_divergence(current, buoyancy_first, 0)
            divergence = divergence + local_divergence(current, buoyancy_second, 1)
            divergence = divergence + local_divergence(current, buoyancy_third, 2)
            change = stiffness * divergence + injection[moment].reshape(NX, NY, NZ)
            following = 2.0 * current - earlier + change
            frame = forward_now[moment].astype(jnp.float32)
            image_sum = image_sum + frame * change
            illumination = illumination + frame * frame
            earlier, current = current, following
        source_pos = source_at.astype(jnp.float32)
        distance = (coord_first - source_pos[0]) ** 2 + (coord_second - source_pos[1]) ** 2 + (coord_third - source_pos[2]) ** 2
        mute_weight = 1.0 - jnp.exp(-distance / (2.0 * MUTE * MUTE))
        return (summed_image + mute_weight * image_sum, summed_light + illumination), (earlier, current)

    start = (jnp.zeros((NX, NY, NZ), jnp.float32), jnp.zeros((NX, NY, NZ), jnp.float32))
    packed = (jnp.arange(GROUPS, dtype=jnp.int32), adjoint_before, adjoint_current, forward_field, source_cell)
    (summed_image, summed_light), (earliers, latests) = lax.scan(one_group, start, packed)
    gradient = summed_image / (summed_light / (STEPS * N_SHOT) + DAMP)
    return gradient.reshape(NX, NY * NZ), earliers, latests
```

```python
import jax
import jax.numpy as jnp
import numpy as np
from jax import lax
from jax.experimental import pallas as pl
from jax.experimental.pallas import tpu as pltpu
from jax.sharding import PartitionSpec as P

MUTE = 6
COEFFS = (1225.0 / 1024.0, -245.0 / 3072.0, 49.0 / 5120.0, -5.0 / 7168.0)
DAMP = 0.1
HALO = 7
SLOTS = 6
FIELDS = 16
F32 = jnp.float32
BF16 = jnp.bfloat16
PARAMS = pltpu.CompilerParams(vmem_limit_bytes=48 * 1024 * 1024)


def shape_of(*dims, dtype=F32):
    return jax.ShapeDtypeStruct(dims, dtype)


def split2(x):
    high = x.astype(BF16)
    return high, (x - high.astype(F32)).astype(BF16)


def split3(x):
    high = x.astype(BF16)
    rest = x - high.astype(F32)
    mid = rest.astype(BF16)
    return high, mid, (rest - mid.astype(F32)).astype(BF16)


def pack_kernel(traces_ref, kernel_ref, target_ref, cell_ref, send_ref):
    rows = traces_ref.shape[0]
    values = jnp.dot(
        traces_ref[...],
        kernel_ref[...],
        precision=lax.Precision.HIGHEST,
        preferred_element_type=F32,
    )
    lane = lax.broadcasted_iota(jnp.int32, (rows, 128), 1)
    hit = target_ref[...] == lane
    onehot = jnp.where(hit, 1.0, 0.0)
    lower = (
        lax.broadcasted_iota(jnp.int32, (rows, rows), 0)
        >= lax.broadcasted_iota(jnp.int32, (rows, rows), 1)
    )
    running = jnp.dot(
        jnp.where(lower, 1.0, 0.0).astype(BF16),
        onehot.astype(BF16),
        preferred_element_type=F32,
    )
    slot = jnp.sum(jnp.where(hit, running, 0.0), axis=1, keepdims=True) - 1.0
    slot = slot.astype(jnp.int32)
    entries = jnp.where(lane % FIELDS == 8, cell_ref[...].astype(F32), values)
    entries = jnp.where(lane // FIELDS == slot, entries, 0.0)
    turned = onehot.T.astype(BF16)
    packed = jnp.zeros((128, 128), F32)
    for piece in split3(entries):
        packed = packed + jnp.dot(turned, piece, preferred_element_type=F32)
    send_ref[...] = packed


def pack(traces, target, cell):
    samples = traces.shape[1]
    position = np.arange(samples, dtype=np.float32)[:, None]
    centers = (np.arange(8, dtype=np.float32)[None, :] + np.float32(0.5)) * np.float32(samples / 8)
    kernel = (0.25 * np.exp(-np.abs(position - centers) / np.float32(samples / 8.0))).astype(np.float32)
    tiled = np.zeros((samples, 128), np.float32)
    for slot in range(SLOTS):
        tiled[:, slot * FIELDS : slot * FIELDS + 8] = kernel
    return pl.pallas_call(
        pack_kernel,
        out_shape=shape_of(128, 128),
        compiler_params=PARAMS,
        name="pack",
    )(traces, jnp.asarray(tiled), target, cell)


def fill_columns(got_ref, spread_ref, moment, nz):
    zlane = lax.broadcasted_iota(jnp.int32, (128, nz), 1)
    for slot in range(SLOTS):
        base = slot * FIELDS
        cell = got_ref[:, base + 8 : base + 9].astype(jnp.int32)
        value = got_ref[:, base + moment : base + moment + 1]
        spread = jnp.where(cell % nz == zlane, value, 0.0)
        high, low = split2(spread)
        spread_ref[0, slot * 128 : (slot + 1) * 128, :] = high
        spread_ref[1, slot * 128 : (slot + 1) * 128, :] = low


def inject_rows(turned_ref, spread_ref, first_row, count, nz):
    row = first_row + lax.broadcasted_iota(jnp.int32, (count, 128), 0)
    picks = []
    for slot in range(SLOTS):
        base = slot * FIELDS
        cell = turned_ref[base + 8 : base + 9, :].astype(jnp.int32)
        picks.append(jnp.where(cell // nz == row, 1.0, 0.0).astype(BF16))
    pick = jnp.concatenate(picks, axis=1)
    return jnp.dot(pick, spread_ref[0], preferred_element_type=F32) + jnp.dot(
        pick, spread_ref[1], preferred_element_type=F32
    )


def first_inject_kernel(got_ref, turned_ref, local_ref, out_ref, spread_ref):
    planes, ny, nz = local_ref.shape
    block = pl.program_id(0)

    @pl.when(block == 0)
    def _():
        fill_columns(got_ref, spread_ref, 0, nz)

    added = inject_rows(turned_ref, spread_ref, block * (planes * ny), planes * ny, nz)
    for x in range(planes):
        out_ref[x] = local_ref[x] + added[x * ny : (x + 1) * ny]


def first_inject(got, turned, local):
    nx, ny, nz = local.shape
    planes = 4
    whole = pl.BlockSpec((128, 128), lambda i: (0, 0))
    field = pl.BlockSpec((planes, ny, nz), lambda i: (i, 0, 0))
    return pl.pallas_call(
        first_inject_kernel,
        grid=(nx // planes,),
        in_specs=[whole, whole, field],
        out_specs=field,
        out_shape=shape_of(nx, ny, nz),
        scratch_shapes=[pltpu.VMEM((2, SLOTS * 128, nz), BF16)],
        compiler_params=PARAMS,
        name="first_inject",
    )(got, turned, local)


def divergence_yz(plane, flux_second, flux_third, ps_ref, qs_ref, index):
    ny, nz = plane.shape
    tiles = nz // 128
    pieces = []
    for tile in range(tiles):
        where = index * tiles + tile
        lanes = slice(tile * 128, (tile + 1) * 128)
        ps_ref[where, 8 : 8 + ny, :] = plane[:, lanes]
        total = None
        for k in range(1, 5):
            term = COEFFS[k - 1] * (
                ps_ref[where, 8 + k : 8 + k + ny, :] - ps_ref[where, 9 - k : 9 - k + ny, :]
            )
            total = term if total is None else total + term
        qs_ref[where, 8 : 8 + ny, :] = flux_second[:, lanes] * total
        total = None
        for k in range(1, 5):
            term = COEFFS[k - 1] * (
                qs_ref[where, 7 + k : 7 + k + ny, :] - qs_ref[where, 8 - k : 8 - k + ny, :]
            )
            total = term if total is None else total + term
        pieces.append(total)
    along_second = jnp.concatenate(pieces, axis=1)

    lane = lax.broadcasted_iota(jnp.int32, (ny, nz), 1)

    def shifted(value, amount):
        if amount == 0:
            return value
        moved = pltpu.roll(value, (-amount) % nz, 1)
        inside = lane < nz - amount if amount > 0 else lane >= -amount
        return jnp.where(inside, moved, 0.0)

    total = None
    for k in range(1, 5):
        term = COEFFS[k - 1] * (shifted(plane, k) - shifted(plane, 1 - k))
        total = term if total is None else total + term
    flux = flux_third * total
    total = None
    for k in range(1, 5):
        term = COEFFS[k - 1] * (shifted(flux, k - 1) - shifted(flux, -k))
        total = term if total is None else total + term
    return along_second + total


def clear_edges(ps_ref, qs_ref, ny):
    zero = jnp.zeros((ps_ref.shape[0], 8, 128), F32)
    for ref in (ps_ref, qs_ref):
        ref[:, 0:8, :] = zero
        ref[:, 8 + ny : 16 + ny, :] = zero


def first_local_kernel(p_ref, k_ref, b2_ref, b3_ref, out_ref, ps_ref, qs_ref):
    planes, ny, nz = p_ref.shape

    @pl.when(pl.program_id(0) == 0)
    def _():
        clear_edges(ps_ref, qs_ref, ny)

    for x in range(planes):
        out_ref[x] = k_ref[x] * divergence_yz(p_ref[x], b2_ref[x], b3_ref[x], ps_ref, qs_ref, x)


def first_local(current, stiffness, b2, b3):
    nx, ny, nz = current.shape
    planes = 4
    field = pl.BlockSpec((planes, ny, nz), lambda i: (i, 0, 0))
    shift = pltpu.VMEM((planes * (nz // 128), ny + 16, 128), F32)
    return pl.pallas_call(
        first_local_kernel,
        grid=(nx // planes,),
        in_specs=[field] * 4,
        out_specs=field,
        out_shape=shape_of(nx, ny, nz),
        scratch_shapes=[shift, shift],
        compiler_params=PARAMS,
        name="first_local",
    )(current, stiffness, b2, b3)


def make_local_kernel(moment):
    def local_kernel(*refs):
        p_ref, k_ref, b2_ref, b3_ref, f_ref, change_ref = refs[:6]
        refs = refs[6:]
        if moment > 1:
            image_ref, refs = refs[0], refs[1:]
        got_ref, turned_ref, out_ref, image_out_ref, ps_ref, qs_ref, spread_ref = refs
        planes, ny, nz = p_ref.shape
        block = pl.program_id(0)

        @pl.when(block == 0)
        def _():
            clear_edges(ps_ref, qs_ref, ny)
            fill_columns(got_ref, spread_ref, moment, nz)

        added = inject_rows(turned_ref, spread_ref, block * (planes * ny), planes * ny, nz)
        for x in range(planes):
            out_ref[x] = (
                k_ref[x] * divergence_yz(p_ref[x], b2_ref[x], b3_ref[x], ps_ref, qs_ref, x)
                + added[x * ny : (x + 1) * ny]
            )
            image = f_ref[0, x].astype(F32) * change_ref[x]
            if moment > 1:
                image = image + image_ref[x]
            image_out_ref[x] = image

    return local_kernel


def local_step(moment, current, stiffness, b2, b3, forward, change, image, got, turned):
    nx, ny, nz = current.shape
    planes = 4
    field = pl.BlockSpec((planes, ny, nz), lambda i: (i, 0, 0))
    frame = pl.BlockSpec((1, planes, ny, nz), lambda i: (moment - 1, i, 0, 0))
    whole = pl.BlockSpec((128, 128), lambda i: (0, 0))
    shift = pltpu.VMEM((planes * (nz // 128), ny + 16, 128), F32)
    images = [image] if moment > 1 else []
    return pl.pallas_call(
        make_local_kernel(moment),
        grid=(nx // planes,),
        in_specs=[field] * 4 + [frame, field] + [field] * len(images) + [whole, whole],
        out_specs=[field, field],
        out_shape=[shape_of(nx, ny, nz)] * 2,
        scratch_shapes=[shift, shift, pltpu.VMEM((2, SLOTS * 128, nz), BF16)],
        compiler_params=PARAMS,
        name="local_step",
    )(current, stiffness, b2, b3, forward, change, *images, got, turned)


def change_column(p_refs, b_refs, k_ref, local_ref, rows):
    pl_ref, pm_ref, pr_ref = p_refs
    bl_ref, bm_ref, br_ref = b_refs
    nx = pm_ref.shape[0]

    def cell(i):
        if i < 0:
            return pl_ref[HALO + i, rows, :]
        if i >= nx:
            return pr_ref[i - nx, rows, :]
        return pm_ref[i, rows, :]

    def face(i):
        if i < 0:
            return bl_ref[4 + i, rows, :]
        if i >= nx:
            return br_ref[i - nx, rows, :]
        return bm_ref[i, rows, :]

    cells = {i: cell(i) for i in range(-HALO, 0)}
    fluxes = {}
    for ahead in range(0, nx + HALO):
        cells[ahead] = cell(ahead)
        j = ahead - 4
        if j >= -4:
            total = None
            for k in range(1, 5):
                term = COEFFS[k - 1] * (cells[j + k] - cells[j + 1 - k])
                total = term if total is None else total + term
            fluxes[j] = face(j) * total
        i = j - 3
        if i >= 0:
            total = None
            for k in range(1, 5):
                term = COEFFS[k - 1] * (fluxes[i + k - 1] - fluxes[i - k])
                total = term if total is None else total + term
            yield i, cells[i], local_ref[i, rows, :] + k_ref[i, rows, :] * total


def update_kernel(
    pl_ref, pm_ref, pr_ref, bl_ref, bm_ref, br_ref, k_ref, local_ref, before_ref,
    next_ref, change_ref, head_ref, tail_ref,
):
    nx, ny = pm_ref.shape[:2]
    for band in range(ny // 8):
        rows = slice(band * 8, band * 8 + 8)
        for i, now, change in change_column(
            (pl_ref, pm_ref, pr_ref), (bl_ref, bm_ref, br_ref), k_ref, local_ref, rows
        ):
            following = 2.0 * now - before_ref[i, rows, :] + change
            next_ref[i, rows, :] = following
            change_ref[i, rows, :] = change
            if i < HALO:
                head_ref[i, rows, :] = following
            if i >= nx - HALO:
                tail_ref[i - (nx - HALO), rows, :] = following


def last_kernel(
    place_ref, pl_ref, pm_ref, pr_ref, bl_ref, bm_ref, br_ref, k_ref, local_ref, before_ref,
    image_ref, f_ref, next_ref, muted_ref, kept_ref,
):
    nx, ny, lanes = pm_ref.shape
    second = lax.broadcasted_iota(jnp.int32, (8, lanes), 0).astype(F32)
    third = (pl.program_id(0) * lanes + lax.broadcasted_iota(jnp.int32, (8, lanes), 1)).astype(F32)
    first_at = (place_ref[3] - place_ref[0]).astype(F32)
    second_at = place_ref[1].astype(F32)
    third_at = place_ref[2].astype(F32)
    for band in range(ny // 8):
        rows = slice(band * 8, band * 8 + 8)
        flat = (second + float(band * 8) - second_at) ** 2 + (third - third_at) ** 2
        for i, now, change in change_column(
            (pl_ref, pm_ref, pr_ref), (bl_ref, bm_ref, br_ref), k_ref, local_ref, rows
        ):
            next_ref[i, rows, :] = 2.0 * now - before_ref[i, rows, :] + change
            image = image_ref[i, rows, :] + f_ref[0, i, rows, :].astype(F32) * change
            distance = (first_at + float(i)) ** 2 + flat
            kept_ref[i, rows, :] = (1.0 - jnp.exp(distance * (-1.0 / (2.0 * MUTE * MUTE)))) * image
    for y in range(ny):
        muted_ref[y // 2, y % 2, :, :] = kept_ref[:, y, :]


def update_step(halos, current, b1_halos, b1, stiffness, local, before):
    nx, ny, nz = current.shape

    def tall(depth):
        return pl.BlockSpec((depth, ny, 128), lambda i: (0, 0, i))

    return pl.pallas_call(
        update_kernel,
        grid=(nz // 128,),
        in_specs=[tall(HALO), tall(nx), tall(HALO), tall(4), tall(nx), tall(3)] + [tall(nx)] * 3,
        out_specs=[tall(nx), tall(nx), tall(HALO), tall(HALO)],
        out_shape=[shape_of(nx, ny, nz)] * 2 + [shape_of(HALO, ny, nz)] * 2,
        compiler_params=PARAMS,
        name="update_step",
    )(halos[0], current, halos[1], b1_halos[0], b1, b1_halos[1], stiffness, local, before)


def last_step(place, halos, current, b1_halos, b1, stiffness, local, before, image, forward):
    nx, ny, nz = current.shape
    steps = forward.shape[0]

    def tall(depth):
        return pl.BlockSpec((depth, ny, 128), lambda i, s: (0, 0, i))

    return pl.pallas_call(
        last_kernel,
        grid_spec=pltpu.PrefetchScalarGridSpec(
            num_scalar_prefetch=1,
            grid=(nz // 128,),
            in_specs=[tall(HALO), tall(nx), tall(HALO), tall(4), tall(nx), tall(3)]
            + [tall(nx)] * 4
            + [pl.BlockSpec((1, nx, ny, 128), lambda i, s: (steps - 1, 0, 0, i))],
            out_specs=[
                tall(nx),
                pl.BlockSpec((ny // 2, 2, nx, 128), lambda i, s: (0, 0, 0, i)),
            ],
            scratch_shapes=[pltpu.VMEM((nx, ny, 128), F32)],
        ),
        out_shape=[shape_of(nx, ny, nz), shape_of(ny // 2, 2, nx, nz)],
        compiler_params=PARAMS,
        name="last_step",
    )(
        place, halos[0], current, halos[1], b1_halos[0], b1, b1_halos[1], stiffness, local, before,
        image, forward,
    )


def light_kernel(f_ref, out_ref, kept_ref):
    steps, nx, ny, lanes = f_ref.shape
    for i in range(nx):
        total = jnp.zeros((ny, lanes), F32)
        for t in range(steps):
            frame = f_ref[t, i].astype(F32)
            total = total + frame * frame
        kept_ref[i] = total
    for y in range(ny):
        out_ref[y // 2, y % 2, :, :] = kept_ref[:, y, :]


def light_sum(forward):
    steps, nx, ny, nz = forward.shape
    return pl.pallas_call(
        light_kernel,
        grid=(nz // 128,),
        in_specs=[pl.BlockSpec((steps, nx, ny, 128), lambda i: (0, 0, 0, i))],
        out_specs=pl.BlockSpec((ny // 2, 2, nx, 128), lambda i: (0, 0, 0, i)),
        out_shape=shape_of(ny // 2, 2, nx, nz),
        scratch_shapes=[pltpu.VMEM((nx, ny, 128), F32)],
        compiler_params=PARAMS,
        name="light_sum",
    )(forward)


def quotient_kernel(image_ref, light_ref, out_ref, *, scale):
    nz = image_ref.shape[-1]
    for side in range(2):
        image = image_ref[0, side]
        light = light_ref[0, side]
        for shot in range(1, image_ref.shape[0]):
            image = image + image_ref[shot, side]
            light = light + light_ref[shot, side]
        out_ref[:, side * nz : (side + 1) * nz] = image / (light * scale + DAMP)


def quotient(images, lights, scale):
    _, _, nx, nz = images.shape
    return pl.pallas_call(
        lambda *refs: quotient_kernel(*refs, scale=scale),
        out_shape=shape_of(nx, 2 * nz),
        compiler_params=PARAMS,
        name="quotient",
    )(images, lights)


def exchange(head, tail):
    count = lax.axis_size("sub")
    from_left = lax.ppermute(tail, "sub", [(i, i + 1) for i in range(count - 1)])
    from_right = lax.ppermute(head, "sub", [(i + 1, i) for i in range(count - 1)])
    return from_left, from_right


def local(
    stiffness, b1, b2, b3, adjoint_before, adjoint_current, forward_field,
    traces, receiver_target, receiver_cell, source_cell,
):
    both = ("shot", "sub")
    steps = forward_field.shape[1]
    nx = stiffness.shape[0]
    forward = forward_field[0]
    before = adjoint_before[0]
    current = adjoint_current[0]

    halos = exchange(current[:HALO], current[nx - HALO :])
    b1_halos = exchange(b1[:3], b1[nx - 4 :])
    send = pack(traces, receiver_target, receiver_cell[:, None])
    got = lax.all_to_all(send, both, split_axis=0, concat_axis=0, tiled=True)
    lights = lax.all_to_all(light_sum(forward), "shot", split_axis=0, concat_axis=0, tiled=True)
    nearby = first_local(current, stiffness, b2, b3)
    turned = got.T
    nearby = first_inject(got, turned, nearby)

    image = None
    for moment in range(steps - 1):
        following, change, head, tail = update_step(
            halos, current, b1_halos, b1, stiffness, nearby, before
        )
        halos = exchange(head, tail)
        before, current = current, following
        nearby, image = local_step(
            moment + 1, current, stiffness, b2, b3, forward, change, image, got, turned
        )
    place = jnp.concatenate(
        [source_cell[0], (lax.axis_index("sub") * nx).astype(jnp.int32)[None]]
    )
    following, muted = last_step(
        place, halos, current, b1_halos, b1, stiffness, nearby, before, image, forward
    )
    images = lax.all_to_all(muted, "shot", split_axis=0, concat_axis=0, tiled=True)
    gradient = quotient(images, lights, 1.0 / (steps * lax.axis_size("shot")))
    return gradient, current[None], following[None]


def solution(mesh):
    placed = (
        P("sub", None, None),
        P("sub", None, None),
        P("sub", None, None),
        P("sub", None, None),
        P("shot", "sub", None, None),
        P("shot", "sub", None, None),
        P("shot", None, "sub", None, None),
        P(("shot", "sub"), None),
        P(("shot", "sub"), None),
        P(("shot", "sub")),
        P("shot", None),
    )
    return jax.shard_map(
        local,
        mesh=mesh,
        in_specs=placed,
        out_specs=(P("sub", "shot"), P("shot", "sub", None, None), P("shot", "sub", None, None)),
        check_vma=False,
    )
```

```python
import jax
import jax.numpy as jnp
import numpy as np
from jax import lax
from jax.experimental import pallas as pl
from jax.experimental.pallas import tpu as pltpu
from jax.sharding import PartitionSpec as P

MUTE = 6
COEFFS = (1225.0 / 1024.0, -245.0 / 3072.0, 49.0 / 5120.0, -5.0 / 7168.0)
DAMP = 0.1
HALO = 7
SLOTS = 6
FIELDS = 16
F32 = jnp.float32
BF16 = jnp.bfloat16
PARAMS = pltpu.CompilerParams(vmem_limit_bytes=10 * 1024 * 1024)


def shape_of(*dims, dtype=F32):
    return jax.ShapeDtypeStruct(dims, dtype)


def split2(x):
    high = x.astype(BF16)
    return high, (x - high.astype(F32)).astype(BF16)


def split3(x):
    high = x.astype(BF16)
    rest = x - high.astype(F32)
    mid = rest.astype(BF16)
    return high, mid, (rest - mid.astype(F32)).astype(BF16)


def contract_last(left, right, **kwargs):
    return lax.dot_general(
        left, right, (((1,), (1,)), ((), ())), preferred_element_type=F32, **kwargs
    )


def prep_kernel(
    traces_ref, kernel_ref, target_ref, cell_ref, p_ref, b_ref,
    send_ref, right_ref, left_ref, sems, *, nz,
):
    nx = p_ref.shape[0]
    copies = [
        pltpu.make_async_copy(p_ref.at[pl.ds(nx - HALO, HALO)], right_ref.at[pl.ds(0, HALO)], sems.at[0]),
        pltpu.make_async_copy(b_ref.at[pl.ds(nx - 4, 4)], right_ref.at[pl.ds(HALO, 4)], sems.at[1]),
        pltpu.make_async_copy(p_ref.at[pl.ds(0, HALO)], left_ref.at[pl.ds(0, HALO)], sems.at[2]),
        pltpu.make_async_copy(b_ref.at[pl.ds(0, 3)], left_ref.at[pl.ds(HALO, 3)], sems.at[3]),
    ]
    for copy in copies:
        copy.start()
    rows = traces_ref.shape[0]
    values = contract_last(kernel_ref[...], traces_ref[...], precision=lax.Precision.HIGHEST)
    lane = lax.broadcasted_iota(jnp.int32, (128, rows), 0)
    hit = target_ref[...] == lane
    onehot = jnp.where(hit, 1.0, 0.0)
    upper = (
        lax.broadcasted_iota(jnp.int32, (rows, rows), 0)
        <= lax.broadcasted_iota(jnp.int32, (rows, rows), 1)
    )
    running = jnp.dot(
        onehot.astype(BF16),
        jnp.where(upper, 1.0, 0.0).astype(BF16),
        preferred_element_type=F32,
    )
    slot = (jnp.sum(jnp.where(hit, running, 0.0), axis=0, keepdims=True) - 1.0).astype(jnp.int32)
    cell = cell_ref[...]
    entries = jnp.where(lane % FIELDS == 8, (cell // nz).astype(F32), values)
    entries = jnp.where(lane % FIELDS == 9, (cell % nz).astype(F32), entries)
    entries = jnp.where(lane // FIELDS == slot, entries, 0.0)
    packed = jnp.zeros((128, 128), F32)
    for piece in split3(entries):
        packed = packed + contract_last(onehot.astype(BF16), piece)
    send_ref[...] = packed
    for copy in copies:
        copy.wait()


def prep(traces, target, cell, current, b1):
    nx, ny, nz = current.shape
    samples = traces.shape[1]
    position = np.arange(samples, dtype=np.float32)[None, :]
    centers = (np.arange(8, dtype=np.float32)[:, None] + np.float32(0.5)) * np.float32(samples / 8)
    kernel = (0.25 * np.exp(-np.abs(position - centers) / np.float32(samples / 8.0))).astype(np.float32)
    tiled = np.zeros((128, samples), np.float32)
    for slot in range(SLOTS):
        tiled[slot * FIELDS : slot * FIELDS + 8] = kernel
    vmem = pl.BlockSpec(memory_space=pltpu.VMEM)
    far = pl.BlockSpec(memory_space=pl.ANY)
    return pl.pallas_call(
        lambda *refs: prep_kernel(*refs, nz=nz),
        in_specs=[vmem] * 4 + [far] * 2,
        out_specs=[vmem] * 3,
        out_shape=[shape_of(128, 128), shape_of(HALO + 4, ny, nz), shape_of(HALO + 3, ny, nz)],
        scratch_shapes=[pltpu.SemaphoreType.DMA((4,))],
        compiler_params=PARAMS,
        name="prep",
    )(traces, jnp.asarray(tiled), target, cell, current, b1)


def fill_columns(got_ref, spread_ref, moment, nz):
    zlane = lax.broadcasted_iota(jnp.int32, (128, nz), 1)
    for slot in range(SLOTS):
        base = slot * FIELDS
        third = got_ref[:, base + 9 : base + 10].astype(jnp.int32)
        value = got_ref[:, base + moment : base + moment + 1]
        spread = jnp.where(third == zlane, value, 0.0)
        high, low = split2(spread)
        spread_ref[0, slot * 128 : (slot + 1) * 128, :] = high
        spread_ref[1, slot * 128 : (slot + 1) * 128, :] = low


def inject_rows(turned, spread_ref, first_row, count):
    row = first_row + lax.broadcasted_iota(jnp.int32, (count, 128), 0)
    picks = []
    for slot in range(SLOTS):
        base = slot * FIELDS
        line = turned[base + 8 : base + 9, :].astype(jnp.int32)
        picks.append(jnp.where(line == row, 1.0, 0.0).astype(BF16))
    pick = jnp.concatenate(picks, axis=1)
    return jnp.dot(pick, spread_ref[0], preferred_element_type=F32) + jnp.dot(
        pick, spread_ref[1], preferred_element_type=F32
    )


GROUP = 4


def inject_group(turned, spread_ref, out_ref, start, base_ref):
    ny = out_ref.shape[1]
    added = inject_rows(turned, spread_ref, start * ny, GROUP * ny)
    for x in range(GROUP):
        piece = added[x * ny : (x + 1) * ny]
        out_ref[start + x] = piece if base_ref is None else base_ref[start + x] + piece


def first_inject_kernel(got_ref, local_ref, out_ref, turned_ref, spread_ref):
    nx, ny, nz = local_ref.shape
    turned_ref[...] = got_ref[...].T
    fill_columns(got_ref, spread_ref, 0, nz)
    turned = turned_ref[...]
    for start in range(0, nx, GROUP):
        inject_group(turned, spread_ref, out_ref, start, local_ref)


def first_inject(got, local):
    nx, ny, nz = local.shape
    return pl.pallas_call(
        first_inject_kernel,
        out_shape=[shape_of(nx, ny, nz), shape_of(128, 128)],
        scratch_shapes=[pltpu.VMEM((2, SLOTS * 128, nz), BF16)],
        compiler_params=PARAMS,
        name="first_inject",
    )(got, local)


def weighted(pairs):
    total = None
    for k, (ahead, behind) in enumerate(pairs):
        term = COEFFS[k] * (ahead - behind)
        total = term if total is None else total + term
    return total


def along_lanes(tiles, amount, lane):
    if amount == 0:
        return tiles
    count = len(tiles)
    turned = [pltpu.roll(tile, (-amount) % 128, 1) for tile in tiles]
    zero = jnp.zeros_like(tiles[0])
    if amount > 0:
        keep = lane < 128 - amount
        return [
            jnp.where(keep, turned[c], turned[c + 1] if c + 1 < count else zero)
            for c in range(count)
        ]
    keep = lane >= -amount
    return [jnp.where(keep, turned[c], turned[c - 1] if c else zero) for c in range(count)]


def third_derivative(tiles, offset, lane):
    moved = {d: along_lanes(tiles, d, lane) for d in range(offset - 4, offset + 4)}
    return [
        weighted([(moved[offset - 1 + k][c], moved[offset - k][c]) for k in range(1, 5)])
        for c in range(len(tiles))
    ]


def second_derivative(ref, where, first, ny):
    return weighted(
        [
            (
                ref[where, 7 + first + k : 7 + first + k + ny, :],
                ref[where, 8 + first - k : 8 + first - k + ny, :],
            )
            for k in range(1, 5)
        ]
    )


def divergence_plane(p_ref, b2_ref, b3_ref, x, ps_ref, qs_ref, index):
    ny, nz = p_ref.shape[1:]
    count = nz // 128
    lane = lax.broadcasted_iota(jnp.int32, (8, 128), 1)
    across = []
    for c in range(count):
        where = index * count + c
        lanes = slice(c * 128, c * 128 + 128)
        ps_ref[where, 8 : 8 + ny, :] = p_ref[x, :, lanes]
        qs_ref[where, 8 : 8 + ny, :] = b2_ref[x, :, lanes] * second_derivative(ps_ref, where, 1, ny)
        across.append(second_derivative(qs_ref, where, 0, ny))
    for band in range(ny // 8):
        rows = slice(band * 8, band * 8 + 8)
        tiles = [p_ref[x, rows, c * 128 : c * 128 + 128] for c in range(count)]
        faces = third_derivative(tiles, 1, lane)
        faces = [faces[c] * b3_ref[x, rows, c * 128 : c * 128 + 128] for c in range(count)]
        along = third_derivative(faces, 0, lane)
        for c in range(count):
            yield rows, slice(c * 128, c * 128 + 128), across[c][rows] + along[c]


def clear_edges(ps_ref, qs_ref, ny):
    zero = jnp.zeros((ps_ref.shape[0], 8, 128), F32)
    for ref in (ps_ref, qs_ref):
        ref[:, 0:8, :] = zero
        ref[:, 8 + ny : 16 + ny, :] = zero


def first_local_kernel(p_ref, k_ref, b2_ref, b3_ref, out_ref, ps_ref, qs_ref):
    nx, ny, nz = p_ref.shape
    clear_edges(ps_ref, qs_ref, ny)

    def planes(group, carry):
        for index in range(GROUP):
            x = group * GROUP + index
            for rows, lanes, total in divergence_plane(p_ref, b2_ref, b3_ref, x, ps_ref, qs_ref, index):
                out_ref[x, rows, lanes] = k_ref[x, rows, lanes] * total
        return carry

    lax.fori_loop(0, nx // GROUP, planes, 0)


def shift_scratch(ny, nz):
    return pltpu.VMEM((GROUP * (nz // 128), ny + 16, 128), F32)


def first_local(current, stiffness, b2, b3):
    nx, ny, nz = current.shape
    return pl.pallas_call(
        first_local_kernel,
        out_shape=shape_of(nx, ny, nz),
        scratch_shapes=[shift_scratch(ny, nz)] * 2,
        compiler_params=PARAMS,
        name="first_local",
    )(current, stiffness, b2, b3)


def make_local_kernel(moment):
    def local_kernel(*refs):
        p_ref, k_ref, b2_ref, b3_ref, f_ref, change_ref = refs[:6]
        refs = refs[6:]
        if moment > 1:
            image_ref, refs = refs[0], refs[1:]
        got_ref, turned_ref, out_ref, image_out_ref, ps_ref, qs_ref, spread_ref, add_ref = refs
        nx, ny, nz = p_ref.shape
        clear_edges(ps_ref, qs_ref, ny)
        fill_columns(got_ref, spread_ref, moment, nz)
        turned = turned_ref[...]

        def planes(group, carry):
            added = inject_rows(turned, spread_ref, group * (GROUP * ny), GROUP * ny)
            add_ref[...] = added
            for index in range(GROUP):
                x = group * GROUP + index
                for rows, lanes, total in divergence_plane(p_ref, b2_ref, b3_ref, x, ps_ref, qs_ref, index):
                    low = index * ny + rows.start
                    out_ref[x, rows, lanes] = k_ref[x, rows, lanes] * total + add_ref[low : low + 8, lanes]
                image = f_ref[moment - 1, x].astype(F32) * change_ref[x]
                if moment > 1:
                    image = image + image_ref[x]
                image_out_ref[x] = image
            return carry

        lax.fori_loop(0, nx // GROUP, planes, 0)

    return local_kernel


def local_step(moment, current, stiffness, b2, b3, forward, change, image, got, turned):
    nx, ny, nz = current.shape
    images = [image] if moment > 1 else []
    return pl.pallas_call(
        make_local_kernel(moment),
        out_shape=[shape_of(nx, ny, nz)] * 2,
        scratch_shapes=[shift_scratch(ny, nz)] * 2
        + [pltpu.VMEM((2, SLOTS * 128, nz), BF16), pltpu.VMEM((GROUP * ny, nz), F32)],
        compiler_params=PARAMS,
        name="local_step",
    )(current, stiffness, b2, b3, forward, change, *images, got, turned)


def change_column(p_refs, b_refs, k_ref, local_ref, rows, lanes):
    pl_ref, pm_ref, pr_ref = p_refs
    bl_ref, bm_ref, br_ref = b_refs
    nx = pm_ref.shape[0]

    def cell(i):
        if i < 0:
            return pl_ref[HALO + i, rows, lanes]
        if i >= nx:
            return pr_ref[i - nx, rows, lanes]
        return pm_ref[i, rows, lanes]

    def face(i):
        if i < 0:
            return bl_ref[HALO + 4 + i, rows, lanes]
        if i >= nx:
            return br_ref[HALO + i - nx, rows, lanes]
        return bm_ref[i, rows, lanes]

    cells = {i: cell(i) for i in range(-HALO, 0)}
    fluxes = {}
    for ahead in range(0, nx + HALO):
        cells[ahead] = cell(ahead)
        j = ahead - 4
        if j >= -4:
            fluxes[j] = face(j) * weighted([(cells[j + k], cells[j + 1 - k]) for k in range(1, 5)])
        i = j - 3
        if i >= 0:
            total = weighted([(fluxes[i + k - 1], fluxes[i - k]) for k in range(1, 5)])
            yield i, cells[i], local_ref[i, rows, lanes] + k_ref[i, rows, lanes] * total


def columns(ny, nz):
    for band in range(ny // 8):
        for c in range(nz // 128):
            yield slice(band * 8, band * 8 + 8), slice(c * 128, c * 128 + 128)


def update_kernel(
    pl_ref, pm_ref, pr_ref, bl_ref, bm_ref, br_ref, k_ref, local_ref, before_ref,
    next_ref, change_ref, head_ref, tail_ref,
):
    nx, ny, nz = pm_ref.shape
    for rows, lanes in columns(ny, nz):
        for i, now, change in change_column(
            (pl_ref, pm_ref, pr_ref), (bl_ref, bm_ref, br_ref), k_ref, local_ref, rows, lanes
        ):
            following = 2.0 * now - before_ref[i, rows, lanes] + change
            next_ref[i, rows, lanes] = following
            change_ref[i, rows, lanes] = change
            if i < HALO:
                head_ref[i, rows, lanes] = following
            if i >= nx - HALO:
                tail_ref[i - (nx - HALO), rows, lanes] = following


def last_kernel(
    place_ref, first_ref, pl_ref, pm_ref, pr_ref, bl_ref, bm_ref, br_ref, k_ref, local_ref,
    before_ref, image_ref, f_ref, next_ref, muted_ref, kept_ref,
):
    nx, ny, nz = pm_ref.shape
    steps = f_ref.shape[0]
    second = lax.broadcasted_iota(jnp.int32, (8, 128), 0).astype(F32)
    third = lax.broadcasted_iota(jnp.int32, (8, 128), 1).astype(F32)
    first_at = (first_ref[0] - place_ref[0, 0]).astype(F32)
    second_at = place_ref[0, 1].astype(F32)
    third_at = place_ref[0, 2].astype(F32)
    for rows, lanes in columns(ny, nz):
        flat = (second + (float(rows.start) - second_at)) ** 2 + (
            third + (float(lanes.start) - third_at)
        ) ** 2
        for i, now, change in change_column(
            (pl_ref, pm_ref, pr_ref), (bl_ref, bm_ref, br_ref), k_ref, local_ref, rows, lanes
        ):
            next_ref[i, rows, lanes] = 2.0 * now - before_ref[i, rows, lanes] + change
            image = image_ref[i, rows, lanes] + f_ref[steps - 1, i, rows, lanes].astype(F32) * change
            distance = (first_at + float(i)) ** 2 + flat
            kept_ref[i, rows, lanes] = (1.0 - jnp.exp(distance * (-1.0 / (2.0 * MUTE * MUTE)))) * image
    for y in range(ny):
        muted_ref[y // 2, y % 2, :, :] = kept_ref[:, y, :]


def update_step(halos, current, b1_halos, b1, stiffness, local, before):
    nx, ny, nz = current.shape
    return pl.pallas_call(
        update_kernel,
        out_shape=[shape_of(nx, ny, nz)] * 2 + [shape_of(HALO, ny, nz)] * 2,
        compiler_params=PARAMS,
        name="update_step",
    )(halos[0], current, halos[1], b1_halos[0], b1, b1_halos[1], stiffness, local, before)


def last_step(place, first, halos, current, b1_halos, b1, stiffness, local, before, image, forward):
    nx, ny, nz = current.shape
    vmem = pl.BlockSpec(memory_space=pltpu.VMEM)
    smem = pl.BlockSpec(memory_space=pltpu.SMEM)
    return pl.pallas_call(
        last_kernel,
        in_specs=[smem] * 2 + [vmem] * 11,
        out_specs=[vmem] * 2,
        out_shape=[shape_of(nx, ny, nz), shape_of(ny // 2, 2, nx, nz)],
        scratch_shapes=[pltpu.VMEM((nx, ny, nz), F32)],
        compiler_params=PARAMS,
        name="last_step",
    )(
        place, first, halos[0], current, halos[1], b1_halos[0], b1, b1_halos[1], stiffness, local,
        before, image, forward,
    )


def light_kernel(f_ref, out_ref, kept_ref):
    steps, nx, ny, nz = f_ref.shape
    for i in range(nx):
        total = None
        for t in range(steps):
            frame = f_ref[t, i].astype(F32)
            total = frame * frame if total is None else total + frame * frame
        kept_ref[i] = total
    for y in range(ny):
        out_ref[y // 2, y % 2, :, :] = kept_ref[:, y, :]


def light_sum(forward):
    steps, nx, ny, nz = forward.shape
    return pl.pallas_call(
        light_kernel,
        out_shape=shape_of(ny // 2, 2, nx, nz),
        scratch_shapes=[pltpu.VMEM((nx, ny, nz), F32)],
        compiler_params=PARAMS,
        name="light_sum",
    )(forward)


def quotient_kernel(image_ref, light_ref, out_ref, *, scale):
    nz = image_ref.shape[-1]
    for side in range(2):
        image = image_ref[0, side]
        for shot in range(1, image_ref.shape[0]):
            image = image + image_ref[shot, side]
        out_ref[:, side * nz : (side + 1) * nz] = image / (light_ref[0, side] * scale + DAMP)


def quotient(images, light, scale):
    _, _, nx, nz = images.shape
    return pl.pallas_call(
        lambda *refs: quotient_kernel(*refs, scale=scale),
        out_shape=shape_of(nx, 2 * nz),
        compiler_params=PARAMS,
        name="quotient",
    )(images, light)


def exchange(head, tail):
    count = lax.axis_size("sub")
    from_left = lax.ppermute(tail, "sub", [(i, i + 1) for i in range(count - 1)])
    from_right = lax.ppermute(head, "sub", [(i + 1, i) for i in range(count - 1)])
    return from_left, from_right


def local(
    stiffness, b1, b2, b3, adjoint_before, adjoint_current, forward_field,
    traces, receiver_target, receiver_cell, source_cell,
):
    both = ("shot", "sub")
    steps = forward_field.shape[1]
    nx = stiffness.shape[0]
    rows = traces.shape[0]
    forward = forward_field[0]
    before = adjoint_before[0]
    current = adjoint_current[0]

    send, right, left = prep(
        traces, receiver_target.reshape(1, rows), receiver_cell.reshape(1, rows), current, b1
    )
    halos = exchange(left, right)
    b1_halos = halos
    got = lax.all_to_all(send, both, split_axis=0, concat_axis=0, tiled=True)
    light = lax.psum_scatter(light_sum(forward), "shot", scatter_dimension=0, tiled=True)
    nearby = first_local(current, stiffness, b2, b3)
    nearby, turned = first_inject(got, nearby)

    image = None
    for moment in range(steps - 1):
        following, change, head, tail = update_step(
            halos, current, b1_halos, b1, stiffness, nearby, before
        )
        halos = exchange(head, tail)
        before, current = current, following
        nearby, image = local_step(
            moment + 1, current, stiffness, b2, b3, forward, change, image, got, turned
        )
    first = (lax.axis_index("sub") * nx).astype(jnp.int32)[None]
    following, muted = last_step(
        source_cell, first, halos, current, b1_halos, b1, stiffness, nearby, before, image, forward
    )
    images = lax.all_to_all(muted, "shot", split_axis=0, concat_axis=0, tiled=True)
    gradient = quotient(images, light, 1.0 / (steps * lax.axis_size("shot")))
    return gradient, current[None], following[None]


def solution(mesh):
    placed = (
        P("sub", None, None),
        P("sub", None, None),
        P("sub", None, None),
        P("sub", None, None),
        P("shot", "sub", None, None),
        P("shot", "sub", None, None),
        P("shot", None, "sub", None, None),
        P(("shot", "sub"), None),
        P(("shot", "sub"), None),
        P(("shot", "sub")),
        P("shot", None),
    )
    return jax.shard_map(
        local,
        mesh=mesh,
        in_specs=placed,
        out_specs=(P("sub", "shot"), P("shot", "sub", None, None), P("shot", "sub", None, None)),
        check_vma=False,
    )
```

```python
import jax
import jax.numpy as jnp
import ml_dtypes
import numpy as np
from jax import lax
from jax.experimental import pallas as pl
from jax.experimental.pallas import tpu as pltpu
from jax.sharding import PartitionSpec as P

MUTE = 6
COEFFS = (1225.0 / 1024.0, -245.0 / 3072.0, 49.0 / 5120.0, -5.0 / 7168.0)
DAMP = 0.1
HALO = 7
SLOTS = 6
FIELDS = 16
F32 = jnp.float32
BF16 = jnp.bfloat16
PARAMS = pltpu.CompilerParams(vmem_limit_bytes=8 * 1024 * 1024)


def shape_of(*dims, dtype=F32):
    return jax.ShapeDtypeStruct(dims, dtype)


def far_away(*arrays):
    return [pltpu.with_memory_space_constraint(a, pltpu.HBM) for a in arrays]


def split2(x):
    high = x.astype(BF16)
    return high, (x - high.astype(F32)).astype(BF16)


def split3(x):
    high = x.astype(BF16)
    rest = x - high.astype(F32)
    mid = rest.astype(BF16)
    return high, mid, (rest - mid.astype(F32)).astype(BF16)


def contract_last(left, right, **kwargs):
    return lax.dot_general(
        left, right, (((1,), (1,)), ((), ())), preferred_element_type=F32, **kwargs
    )


def prep_kernel(
    traces_far, kernel_far, target_far, cell_far, p_ref, b_ref,
    send_ref, right_ref, left_ref, traces_ref, kernel_ref, target_ref, cell_ref, sems, *, nz,
):
    nx = p_ref.shape[0]
    loads = [
        pltpu.make_async_copy(traces_far, traces_ref, sems.at[0]),
        pltpu.make_async_copy(kernel_far, kernel_ref, sems.at[1]),
        pltpu.make_async_copy(target_far, target_ref, sems.at[2]),
        pltpu.make_async_copy(cell_far, cell_ref, sems.at[3]),
    ]
    copies = [
        pltpu.make_async_copy(p_ref.at[pl.ds(nx - HALO, HALO)], right_ref.at[pl.ds(0, HALO)], sems.at[4]),
        pltpu.make_async_copy(b_ref.at[pl.ds(nx - 4, 4)], right_ref.at[pl.ds(HALO, 4)], sems.at[5]),
        pltpu.make_async_copy(p_ref.at[pl.ds(0, HALO)], left_ref.at[pl.ds(0, HALO)], sems.at[6]),
        pltpu.make_async_copy(b_ref.at[pl.ds(0, 3)], left_ref.at[pl.ds(HALO, 3)], sems.at[7]),
    ]
    for copy in loads + copies:
        copy.start()
    for load in loads:
        load.wait()
    rows = traces_ref.shape[0]
    values = contract_last(kernel_ref[...], traces_ref[...], precision=lax.Precision.HIGHEST)
    lane = lax.broadcasted_iota(jnp.int32, (128, rows), 0)
    hit = target_ref[...] == lane
    onehot = jnp.where(hit, 1.0, 0.0)
    upper = (
        lax.broadcasted_iota(jnp.int32, (rows, rows), 0)
        <= lax.broadcasted_iota(jnp.int32, (rows, rows), 1)
    )
    running = jnp.dot(
        onehot.astype(BF16),
        jnp.where(upper, 1.0, 0.0).astype(BF16),
        preferred_element_type=F32,
    )
    slot = (jnp.sum(jnp.where(hit, running, 0.0), axis=0, keepdims=True) - 1.0).astype(jnp.int32)
    cell = cell_ref[...]
    entries = jnp.where(lane % FIELDS == 8, (cell // nz).astype(F32), values)
    entries = jnp.where(lane % FIELDS == 9, (cell % nz).astype(F32), entries)
    entries = jnp.where(lane // FIELDS == slot, entries, 0.0)
    packed = jnp.zeros((128, 128), F32)
    for piece in split3(entries):
        packed = packed + contract_last(onehot.astype(BF16), piece)
    send_ref[...] = packed
    for copy in copies:
        copy.wait()


def prep(traces, target, cell, current, b1):
    nx, ny, nz = current.shape
    samples = traces.shape[1]
    position = np.arange(samples, dtype=np.float32)[None, :]
    centers = (np.arange(8, dtype=np.float32)[:, None] + np.float32(0.5)) * np.float32(samples / 8)
    kernel = (0.25 * np.exp(-np.abs(position - centers) / np.float32(samples / 8.0))).astype(np.float32)
    tiled = np.zeros((128, samples), np.float32)
    for slot in range(SLOTS):
        tiled[slot * FIELDS : slot * FIELDS + 8] = kernel
    vmem = pl.BlockSpec(memory_space=pltpu.VMEM)
    far = pl.BlockSpec(memory_space=pltpu.HBM)
    return pl.pallas_call(
        lambda *refs: prep_kernel(*refs, nz=nz),
        in_specs=[far] * 6,
        out_specs=[vmem] * 3,
        out_shape=[shape_of(128, 128), shape_of(HALO + 4, ny, nz), shape_of(HALO + 3, ny, nz)],
        scratch_shapes=[
            pltpu.VMEM(traces.shape, F32),
            pltpu.VMEM((128, samples), F32),
            pltpu.VMEM(target.shape, jnp.int32),
            pltpu.VMEM(cell.shape, jnp.int32),
            pltpu.SemaphoreType.DMA((8,)),
        ],
        compiler_params=PARAMS,
        name="prep",
    )(*far_away(traces, jnp.asarray(tiled), target, cell, current, b1))


def fill_columns(got_ref, spread_ref, moment, nz):
    zlane = lax.broadcasted_iota(jnp.int32, (128, nz), 1)
    for slot in range(SLOTS):
        base = slot * FIELDS
        third = got_ref[:, base + 9 : base + 10].astype(jnp.int32)
        value = got_ref[:, base + moment : base + moment + 1]
        spread = jnp.where(third == zlane, value, 0.0)
        high, low = split2(spread)
        spread_ref[0, slot * 128 : (slot + 1) * 128, :] = high
        spread_ref[1, slot * 128 : (slot + 1) * 128, :] = low


def inject_rows(turned, spread_ref, first_row, count):
    row = first_row + lax.broadcasted_iota(jnp.int32, (count, 128), 0)
    picks = []
    for slot in range(SLOTS):
        base = slot * FIELDS
        line = turned[base + 8 : base + 9, :].astype(jnp.int32)
        picks.append(jnp.where(line == row, 1.0, 0.0).astype(BF16))
    pick = jnp.concatenate(picks, axis=1)
    return jnp.dot(pick, spread_ref[0], preferred_element_type=F32) + jnp.dot(
        pick, spread_ref[1], preferred_element_type=F32
    )


def weighted(pairs):
    total = None
    for k, (ahead, behind) in enumerate(pairs):
        term = COEFFS[k] * (ahead - behind)
        total = term if total is None else total + term
    return total


def band_matrices(nz):
    forward = np.zeros((nz, nz), np.float64)
    for face in range(nz):
        for k in range(1, 5):
            if face + k < nz:
                forward[face + k, face] += COEFFS[k - 1]
            if face + 1 - k >= 0:
                forward[face + 1 - k, face] -= COEFFS[k - 1]
    pieces = []
    for matrix in (forward, -forward.T):
        full = matrix.astype(np.float32)
        high = full.astype(ml_dtypes.bfloat16)
        low = (full - high.astype(np.float32)).astype(ml_dtypes.bfloat16)
        pieces += [high, low]
    return np.stack(pieces)


def banded(value, bands_ref, first):
    high, low = split2(value)
    return (
        jnp.dot(high, bands_ref[first], preferred_element_type=F32)
        + jnp.dot(low, bands_ref[first], preferred_element_type=F32)
        + jnp.dot(high, bands_ref[first + 1], preferred_element_type=F32)
    )


def second_derivative(ref, where, first, ny):
    return weighted(
        [
            (
                ref[where, 7 + first + k : 7 + first + k + ny, :],
                ref[where, 8 + first - k : 8 + first - k + ny, :],
            )
            for k in range(1, 5)
        ]
    )


def along_third(p_ref, b3_ref, bands_ref):
    nx, ny, nz = p_ref.shape
    flux = b3_ref[...].reshape(nx * ny, nz) * banded(p_ref[...].reshape(nx * ny, nz), bands_ref, 0)
    return banded(flux, bands_ref, 2)


def along_second(p_ref, b2_ref, x, lanes, ps_ref, qs_ref, where):
    ny = p_ref.shape[1]
    ps_ref[where, 8 : 8 + ny, :] = p_ref[x, :, lanes]
    qs_ref[where, 8 : 8 + ny, :] = b2_ref[x, :, lanes] * second_derivative(ps_ref, where, 1, ny)
    return second_derivative(qs_ref, where, 0, ny)


def local_change(
    p_ref, k_ref, b2_ref, b3_ref, bands_ref, got_ref, turned, moment, out_ref, scratch, and_then=None
):
    ps_ref, qs_ref, spread_ref, added_ref, third_ref = scratch
    nx, ny, nz = p_ref.shape
    clear_edges(ps_ref, qs_ref, ny)
    fill_columns(got_ref, spread_ref, moment, nz)
    added_ref[...] = inject_rows(turned, spread_ref, 0, nx * ny).reshape(nx, ny, nz)
    third_ref[...] = along_third(p_ref, b3_ref, bands_ref).reshape(nx, ny, nz)
    count = nz // 128

    def planes(group, carry):
        for index in range(GROUP):
            x = group * GROUP + index
            for c in range(count):
                lanes = slice(c * 128, c * 128 + 128)
                second = along_second(p_ref, b2_ref, x, lanes, ps_ref, qs_ref, index * count + c)
                out_ref[x, :, lanes] = (
                    k_ref[x, :, lanes] * (second + third_ref[x, :, lanes]) + added_ref[x, :, lanes]
                )
            if and_then is not None:
                and_then(x)
        return carry

    lax.fori_loop(0, nx // GROUP, planes, 0)


def local_scratch(nx, ny, nz):
    return [shift_scratch(ny, nz)] * 2 + [
        pltpu.VMEM((2, SLOTS * 128, nz), BF16),
        pltpu.VMEM((nx, ny, nz), F32),
        pltpu.VMEM((nx, ny, nz), F32),
    ]


def clear_edges(ps_ref, qs_ref, ny):
    zero = jnp.zeros((ps_ref.shape[0], 8, 128), F32)
    for ref in (ps_ref, qs_ref):
        ref[:, 0:8, :] = zero
        ref[:, 8 + ny : 16 + ny, :] = zero


GROUP = 4
LOADS = 5


def first_local_kernel(
    got_ref, p_far, bands_far, k_far, b2_far, b3_far, b1_far, before_far, frames_far,
    out_ref, turned_ref, p_ref, bands_ref, k_ref, b2_ref, b3_ref, b1_ref, before_ref, frames_ref,
    *scratch,
):
    *scratch, sems = scratch
    far = (p_far, bands_far, k_far, b2_far, b3_far, b1_far, before_far, frames_far)
    near = (p_ref, bands_ref, k_ref, b2_ref, b3_ref, b1_ref, before_ref, frames_ref)
    copies = [pltpu.make_async_copy(f, n, sems.at[i]) for i, (f, n) in enumerate(zip(far, near))]
    for copy in copies:
        copy.start()
    turned_ref[...] = got_ref[...].T
    for copy in copies[:LOADS]:
        copy.wait()
    local_change(
        p_ref, k_ref, b2_ref, b3_ref, bands_ref, got_ref, turned_ref[...], 0, out_ref, scratch
    )
    for copy in copies[LOADS:]:
        copy.wait()


def shift_scratch(ny, nz):
    return pltpu.VMEM((GROUP * (nz // 128), ny + 16, 128), F32)


def first_local(got, *arrays):
    nx, ny, nz = arrays[0].shape
    vmem = pl.BlockSpec(memory_space=pltpu.VMEM)
    far = pl.BlockSpec(memory_space=pltpu.HBM)
    return pl.pallas_call(
        first_local_kernel,
        in_specs=[vmem] + [far] * len(arrays),
        out_specs=[vmem] * (2 + len(arrays)),
        out_shape=[shape_of(nx, ny, nz), shape_of(128, 128)]
        + [shape_of(*a.shape, dtype=a.dtype) for a in arrays],
        scratch_shapes=local_scratch(nx, ny, nz) + [pltpu.SemaphoreType.DMA((len(arrays),))],
        compiler_params=PARAMS,
        name="first_local",
    )(got, *far_away(*arrays))


def make_local_kernel(moment):
    def local_kernel(*refs):
        p_ref, bands_ref, k_ref, b2_ref, b3_ref, f_ref, change_ref = refs[:7]
        refs = refs[7:]
        if moment > 1:
            image_ref, refs = refs[0], refs[1:]
            light_ref, refs = refs[0], refs[1:]
        got_ref, turned_ref, out_ref, image_out_ref, light_out_ref, *scratch = refs

        def accumulate(x):
            frame = f_ref[moment - 1, x].astype(F32)
            image = frame * change_ref[x]
            light = frame * frame
            if moment > 1:
                image = image + image_ref[x]
                light = light + light_ref[x]
            if moment == f_ref.shape[0] - 1:
                frame = f_ref[moment, x].astype(F32)
                light = light + frame * frame
            image_out_ref[x] = image
            light_out_ref[x] = light

        local_change(
            p_ref, k_ref, b2_ref, b3_ref, bands_ref, got_ref, turned_ref[...], moment, out_ref,
            scratch, accumulate,
        )

    return local_kernel


def local_step(moment, current, bands, stiffness, b2, b3, frames, change, sums, got, turned):
    nx, ny, nz = current.shape
    images = list(sums) if moment > 1 else []
    return pl.pallas_call(
        make_local_kernel(moment),
        in_specs=[pl.BlockSpec(memory_space=pltpu.VMEM)] * (9 + len(images)),
        out_specs=[pl.BlockSpec(memory_space=pltpu.VMEM)] * 3,
        out_shape=[shape_of(nx, ny, nz)] * 3,
        scratch_shapes=local_scratch(nx, ny, nz),
        compiler_params=PARAMS,
        name="local_step",
    )(current, bands, stiffness, b2, b3, frames, change, *images, got, turned)


def edge_factors(place_ref, nx):
    first = place_ref[3]
    return (
        jnp.where(first > 0, 1.0, 0.0).astype(F32),
        jnp.where(first < place_ref[4], 1.0, 0.0).astype(F32),
    )


def change_column(edges, p_refs, b_refs, k_ref, local_ref, rows, lanes):
    pl_ref, pm_ref, pr_ref = p_refs
    bl_ref, bm_ref, br_ref = b_refs
    nx = pm_ref.shape[0]

    def cell(i):
        if i < 0:
            return edges[0] * pl_ref[HALO + i, rows, lanes]
        if i >= nx:
            return edges[1] * pr_ref[i - nx, rows, lanes]
        return pm_ref[i, rows, lanes]

    def face(i):
        if i < 0:
            return edges[0] * bl_ref[HALO + 4 + i, rows, lanes]
        if i >= nx:
            return edges[1] * br_ref[HALO + i - nx, rows, lanes]
        return bm_ref[i, rows, lanes]

    cells = {i: cell(i) for i in range(-HALO, 0)}
    fluxes = {}
    for ahead in range(0, nx + HALO):
        cells[ahead] = cell(ahead)
        j = ahead - 4
        if j >= -4:
            fluxes[j] = face(j) * weighted([(cells[j + k], cells[j + 1 - k]) for k in range(1, 5)])
        i = j - 3
        if i >= 0:
            total = weighted([(fluxes[i + k - 1], fluxes[i - k]) for k in range(1, 5)])
            yield i, cells[i], local_ref[i, rows, lanes] + k_ref[i, rows, lanes] * total


def each_column(ny, nz, work):
    def band(index, carry):
        for c in range(nz // 128):
            work(pl.ds(pl.multiple_of(index * 8, 8), 8), slice(c * 128, c * 128 + 128), index, c)
        return carry

    lax.fori_loop(0, ny // 8, band, 0)


def update_kernel(
    place_ref, pl_ref, pm_ref, pr_ref, bl_ref, bm_ref, br_ref, k_ref, local_ref, before_ref,
    next_ref, change_ref, head_ref, tail_ref,
):
    nx, ny, nz = pm_ref.shape
    edges = edge_factors(place_ref, nx)

    def work(rows, lanes, band, tile):
        for i, now, change in change_column(
            edges, (pl_ref, pm_ref, pr_ref), (bl_ref, bm_ref, br_ref), k_ref, local_ref, rows, lanes
        ):
            following = 2.0 * now - before_ref[i, rows, lanes] + change
            next_ref[i, rows, lanes] = following
            change_ref[i, rows, lanes] = change
            if i < HALO:
                head_ref[i, rows, lanes] = following
            if i >= nx - HALO:
                tail_ref[i - (nx - HALO), rows, lanes] = following

    each_column(ny, nz, work)


def last_kernel(
    place_ref, pl_ref, pm_ref, pr_ref, bl_ref, bm_ref, br_ref, k_ref, local_ref,
    before_ref, image_ref, f_ref, light_ref, next_ref, muted_ref, kept_ref,
):
    nx, ny, nz = pm_ref.shape
    steps = f_ref.shape[0]
    edges = edge_factors(place_ref, nx)
    second = lax.broadcasted_iota(jnp.int32, (8, 128), 0).astype(F32)
    third = lax.broadcasted_iota(jnp.int32, (8, 128), 1).astype(F32)
    first_at = (place_ref[3] - place_ref[0]).astype(F32)
    second_at = place_ref[1].astype(F32)
    third_at = place_ref[2].astype(F32)

    def work(rows, lanes, band, tile):
        flat = (second + ((band * 8).astype(F32) - second_at)) ** 2 + (
            third + (float(tile * 128) - third_at)
        ) ** 2
        for i, now, change in change_column(
            edges, (pl_ref, pm_ref, pr_ref), (bl_ref, bm_ref, br_ref), k_ref, local_ref, rows, lanes
        ):
            next_ref[i, rows, lanes] = 2.0 * now - before_ref[i, rows, lanes] + change
            image = image_ref[i, rows, lanes] + f_ref[steps - 1, i, rows, lanes].astype(F32) * change
            distance = (first_at + float(i)) ** 2 + flat
            kept_ref[i, rows, lanes] = (1.0 - jnp.exp(distance * (-1.0 / (2.0 * MUTE * MUTE)))) * image

    each_column(ny, nz, work)
    for y in range(ny):
        muted_ref[y // 2, y % 2, :, :] = kept_ref[:, y, :]
        muted_ref[y // 2, 2 + y % 2, :, :] = light_ref[:, y, :]


def update_step(place, halos, current, b1_halos, b1, stiffness, local, before):
    nx, ny, nz = current.shape
    return pl.pallas_call(
        update_kernel,
        in_specs=[pl.BlockSpec(memory_space=pltpu.SMEM)] + [pl.BlockSpec(memory_space=pltpu.VMEM)] * 9,
        out_specs=[pl.BlockSpec(memory_space=pltpu.VMEM)] * 4,
        out_shape=[shape_of(nx, ny, nz)] * 2 + [shape_of(HALO, ny, nz)] * 2,
        compiler_params=PARAMS,
        name="update_step",
    )(place, halos[0], current, halos[1], b1_halos[0], b1, b1_halos[1], stiffness, local, before)


def last_step(place, halos, current, b1_halos, b1, stiffness, local, before, image, forward, light):
    nx, ny, nz = current.shape
    vmem = pl.BlockSpec(memory_space=pltpu.VMEM)
    smem = pl.BlockSpec(memory_space=pltpu.SMEM)
    return pl.pallas_call(
        last_kernel,
        in_specs=[smem] + [vmem] * 12,
        out_specs=[vmem] * 2,
        out_shape=[shape_of(nx, ny, nz), shape_of(ny // 2, 4, nx, nz)],
        scratch_shapes=[pltpu.VMEM((nx, ny, nz), F32)],
        compiler_params=PARAMS,
        name="last_step",
    )(
        place, halos[0], current, halos[1], b1_halos[0], b1, b1_halos[1], stiffness, local,
        before, image, forward, light,
    )


def quotient_kernel(image_ref, out_ref, *, scale):
    nz = image_ref.shape[-1]
    for side in range(2):
        image = image_ref[0, side]
        light = image_ref[0, 2 + side]
        for shot in range(1, image_ref.shape[0]):
            image = image + image_ref[shot, side]
            light = light + image_ref[shot, 2 + side]
        out_ref[:, side * nz : (side + 1) * nz] = image / (light * scale + DAMP)


def quotient(images, scale):
    _, _, nx, nz = images.shape
    return pl.pallas_call(
        lambda *refs: quotient_kernel(*refs, scale=scale),
        out_shape=shape_of(nx, 2 * nz),
        compiler_params=PARAMS,
        name="quotient",
    )(images)


def exchange(head, tail):
    count = lax.axis_size("sub")
    from_left = lax.ppermute(tail, "sub", [(i, (i + 1) % count) for i in range(count)])
    from_right = lax.ppermute(head, "sub", [((i + 1) % count, i) for i in range(count)])
    return from_left, from_right


def local(
    stiffness, b1, b2, b3, adjoint_before, adjoint_current, forward_field,
    traces, receiver_target, receiver_cell, source_cell,
):
    both = ("shot", "sub")
    steps = forward_field.shape[1]
    nx = stiffness.shape[0]
    rows = traces.shape[0]
    forward = forward_field[0]
    before = adjoint_before[0]
    current = adjoint_current[0]

    nx_all = nx * lax.axis_size("sub")
    place = jnp.concatenate(
        [
            source_cell[0],
            (lax.axis_index("sub") * nx).astype(jnp.int32)[None],
            jnp.full((1,), nx_all - nx, jnp.int32),
        ]
    )
    send, right, left = prep(
        traces, receiver_target.reshape(1, rows), receiver_cell.reshape(1, rows), current, b1
    )
    got = lax.all_to_all(send, both, split_axis=0, concat_axis=0, tiled=True)
    halos = exchange(left, right)
    b1_halos = halos
    got, place = lax.optimization_barrier((got, place))
    bands = jnp.asarray(band_matrices(current.shape[2]))
    nearby, turned, current, bands, stiffness, b2, b3, b1, before, frames = first_local(
        got, current, bands, stiffness, b2, b3, b1, before, forward
    )

    image = light = None
    for moment in range(steps - 1):
        following, change, head, tail = update_step(
            place, halos, current, b1_halos, b1, stiffness, nearby, before
        )
        halos = exchange(head, tail)
        before, current = current, following
        nearby, image, light = local_step(
            moment + 1, current, bands, stiffness, b2, b3, frames, change, (image, light), got, turned
        )
    following, sums = last_step(
        place, halos, current, b1_halos, b1, stiffness, nearby, before, image, frames, light
    )
    sums = lax.all_to_all(sums, "shot", split_axis=0, concat_axis=0, tiled=True)
    gradient = quotient(sums, 1.0 / (steps * lax.axis_size("shot")))
    return gradient, current[None], following[None]


def solution(mesh):
    placed = (
        P("sub", None, None),
        P("sub", None, None),
        P("sub", None, None),
        P("sub", None, None),
        P("shot", "sub", None, None),
        P("shot", "sub", None, None),
        P("shot", None, "sub", None, None),
        P(("shot", "sub"), None),
        P(("shot", "sub"), None),
        P(("shot", "sub")),
        P("shot", None),
    )
    return jax.shard_map(
        local,
        mesh=mesh,
        in_specs=placed,
        out_specs=(P("sub", "shot"), P("shot", "sub", None, None), P("shot", "sub", None, None)),
        check_vma=False,
    )
```

```python
import jax
import jax.numpy as jnp
import numpy as np
from jax import lax
from jax.experimental import pallas as pl
from jax.experimental.pallas import tpu as pltpu
from jax.sharding import PartitionSpec as P

MUTE = 6
COEFFS = (1225.0 / 1024.0, -245.0 / 3072.0, 49.0 / 5120.0, -5.0 / 7168.0)
DAMP = 0.1
HALO = 7
SLOTS = 6
FIELDS = 16
F32 = jnp.float32
BF16 = jnp.bfloat16
PARAMS = pltpu.CompilerParams(vmem_limit_bytes=8 * 1024 * 1024)


def shape_of(*dims, dtype=F32):
    return jax.ShapeDtypeStruct(dims, dtype)


def far_away(*arrays):
    return [pltpu.with_memory_space_constraint(a, pltpu.HBM) for a in arrays]


def split2(x):
    high = x.astype(BF16)
    return high, (x - high.astype(F32)).astype(BF16)


def split3(x):
    high = x.astype(BF16)
    rest = x - high.astype(F32)
    mid = rest.astype(BF16)
    return high, mid, (rest - mid.astype(F32)).astype(BF16)


def contract_last(left, right, **kwargs):
    return lax.dot_general(
        left, right, (((1,), (1,)), ((), ())), preferred_element_type=F32, **kwargs
    )


def prep_kernel(
    traces_far, kernel_far, target_far, cell_far, p_ref, b_ref,
    send_ref, right_ref, left_ref, traces_ref, kernel_ref, target_ref, cell_ref, sems, *, nz,
):
    nx = p_ref.shape[0]
    loads = [
        pltpu.make_async_copy(traces_far, traces_ref, sems.at[0]),
        pltpu.make_async_copy(kernel_far, kernel_ref, sems.at[1]),
        pltpu.make_async_copy(target_far, target_ref, sems.at[2]),
        pltpu.make_async_copy(cell_far, cell_ref, sems.at[3]),
    ]
    copies = [
        pltpu.make_async_copy(p_ref.at[pl.ds(nx - HALO, HALO)], right_ref.at[pl.ds(0, HALO)], sems.at[4]),
        pltpu.make_async_copy(b_ref.at[pl.ds(nx - 4, 4)], right_ref.at[pl.ds(HALO, 4)], sems.at[5]),
        pltpu.make_async_copy(p_ref.at[pl.ds(0, HALO)], left_ref.at[pl.ds(0, HALO)], sems.at[6]),
        pltpu.make_async_copy(b_ref.at[pl.ds(0, 3)], left_ref.at[pl.ds(HALO, 3)], sems.at[7]),
    ]
    for copy in loads + copies:
        copy.start()
    for load in loads:
        load.wait()
    rows = traces_ref.shape[0]
    values = contract_last(kernel_ref[...], traces_ref[...], precision=lax.Precision.HIGHEST)
    lane = lax.broadcasted_iota(jnp.int32, (128, rows), 0)
    hit = target_ref[...] == lane
    onehot = jnp.where(hit, 1.0, 0.0)
    upper = (
        lax.broadcasted_iota(jnp.int32, (rows, rows), 0)
        <= lax.broadcasted_iota(jnp.int32, (rows, rows), 1)
    )
    running = jnp.dot(
        onehot.astype(BF16),
        jnp.where(upper, 1.0, 0.0).astype(BF16),
        preferred_element_type=F32,
    )
    slot = (jnp.sum(jnp.where(hit, running, 0.0), axis=0, keepdims=True) - 1.0).astype(jnp.int32)
    cell = cell_ref[...]
    entries = jnp.where(lane % FIELDS == 8, (cell // nz).astype(F32), values)
    entries = jnp.where(lane % FIELDS == 9, (cell % nz).astype(F32), entries)
    entries = jnp.where(lane // FIELDS == slot, entries, 0.0)
    packed = jnp.zeros((128, 128), F32)
    for piece in split3(entries):
        packed = packed + contract_last(onehot.astype(BF16), piece)
    send_ref[...] = packed
    for copy in copies:
        copy.wait()


def prep(traces, target, cell, current, b1):
    nx, ny, nz = current.shape
    samples = traces.shape[1]
    position = np.arange(samples, dtype=np.float32)[None, :]
    centers = (np.arange(8, dtype=np.float32)[:, None] + np.float32(0.5)) * np.float32(samples / 8)
    kernel = (0.25 * np.exp(-np.abs(position - centers) / np.float32(samples / 8.0))).astype(np.float32)
    tiled = np.zeros((128, samples), np.float32)
    for slot in range(SLOTS):
        tiled[slot * FIELDS : slot * FIELDS + 8] = kernel
    vmem = pl.BlockSpec(memory_space=pltpu.VMEM)
    far = pl.BlockSpec(memory_space=pltpu.HBM)
    return pl.pallas_call(
        lambda *refs: prep_kernel(*refs, nz=nz),
        in_specs=[far] * 6,
        out_specs=[vmem] * 3,
        out_shape=[shape_of(128, 128), shape_of(HALO + 4, ny, nz), shape_of(HALO + 3, ny, nz)],
        scratch_shapes=[
            pltpu.VMEM(traces.shape, F32),
            pltpu.VMEM((128, samples), F32),
            pltpu.VMEM(target.shape, jnp.int32),
            pltpu.VMEM(cell.shape, jnp.int32),
            pltpu.SemaphoreType.DMA((8,)),
        ],
        compiler_params=PARAMS,
        name="prep",
    )(*far_away(traces, jnp.asarray(tiled), target, cell, current, b1))


def fill_columns(got_ref, spread_ref, moment, nz):
    zlane = lax.broadcasted_iota(jnp.int32, (128, nz), 1)
    for slot in range(SLOTS):
        base = slot * FIELDS
        third = got_ref[:, base + 9 : base + 10].astype(jnp.int32)
        value = got_ref[:, base + moment : base + moment + 1]
        spread = jnp.where(third == zlane, value, 0.0)
        high, low = split2(spread)
        spread_ref[0, slot * 128 : (slot + 1) * 128, :] = high
        spread_ref[1, slot * 128 : (slot + 1) * 128, :] = low


def inject_rows(turned, spread_ref, first_row, count):
    row = first_row + lax.broadcasted_iota(jnp.int32, (count, 128), 0)
    picks = []
    for slot in range(SLOTS):
        base = slot * FIELDS
        line = turned[base + 8 : base + 9, :].astype(jnp.int32)
        picks.append(jnp.where(line == row, 1.0, 0.0).astype(BF16))
    pick = jnp.concatenate(picks, axis=1)
    return jnp.dot(pick, spread_ref[0], preferred_element_type=F32) + jnp.dot(
        pick, spread_ref[1], preferred_element_type=F32
    )


def weighted(pairs):
    total = None
    for k, (ahead, behind) in enumerate(pairs):
        term = COEFFS[k] * (ahead - behind)
        total = term if total is None else total + term
    return total


def fill_bands(bands_ref):
    nz = bands_ref.shape[1]
    gap = lax.broadcasted_iota(jnp.int32, (nz, nz), 0) - lax.broadcasted_iota(
        jnp.int32, (nz, nz), 1
    )
    for side in range(2):
        band = jnp.zeros((nz, nz), F32)
        for k in range(1, 5):
            band = jnp.where(gap == k - side, COEFFS[k - 1], band)
            band = jnp.where(gap == 1 - k - side, -COEFFS[k - 1], band)
        high, low = split2(band)
        bands_ref[2 * side] = high
        bands_ref[2 * side + 1] = low


def banded(value, bands_ref, first):
    high, low = split2(value)
    return (
        jnp.dot(high, bands_ref[first], preferred_element_type=F32)
        + jnp.dot(low, bands_ref[first], preferred_element_type=F32)
        + jnp.dot(high, bands_ref[first + 1], preferred_element_type=F32)
    )


def second_derivative(ref, where, first, ny):
    return weighted(
        [
            (
                ref[where, 7 + first + k : 7 + first + k + ny, :],
                ref[where, 8 + first - k : 8 + first - k + ny, :],
            )
            for k in range(1, 5)
        ]
    )


def along_third(p_ref, b3_ref, bands_ref):
    nx, ny, nz = p_ref.shape
    flux = b3_ref[...].reshape(nx * ny, nz) * banded(p_ref[...].reshape(nx * ny, nz), bands_ref, 0)
    return banded(flux, bands_ref, 2)


def along_second(p_ref, b2_ref, x, lanes, ps_ref, qs_ref, where):
    ny = p_ref.shape[1]
    ps_ref[where, 8 : 8 + ny, :] = p_ref[x, :, lanes]
    qs_ref[where, 8 : 8 + ny, :] = b2_ref[x, :, lanes] * second_derivative(ps_ref, where, 1, ny)
    return second_derivative(qs_ref, where, 0, ny)


def local_change(
    p_ref, k_ref, b2_ref, b3_ref, bands_ref, got_ref, turned, moment, out_ref, scratch, and_then=None
):
    ps_ref, qs_ref, third_ref, *more = scratch
    nx, ny, nz = p_ref.shape
    clear_edges(ps_ref, qs_ref, ny)
    if got_ref is not None:
        spread_ref, added_ref = more
        fill_columns(got_ref, spread_ref, moment, nz)
        added_ref[...] = inject_rows(turned, spread_ref, 0, nx * ny).reshape(nx, ny, nz)
    third_ref[...] = along_third(p_ref, b3_ref, bands_ref).reshape(nx, ny, nz)
    count = nz // 128

    def planes(group, carry):
        for index in range(GROUP):
            x = group * GROUP + index
            for c in range(count):
                lanes = slice(c * 128, c * 128 + 128)
                second = along_second(p_ref, b2_ref, x, lanes, ps_ref, qs_ref, index * count + c)
                value = k_ref[x, :, lanes] * (second + third_ref[x, :, lanes])
                if got_ref is not None:
                    value = value + added_ref[x, :, lanes]
                out_ref[x, :, lanes] = value
            if and_then is not None:
                and_then(x)
        return carry

    lax.fori_loop(0, nx // GROUP, planes, 0)


def local_scratch(nx, ny, nz, injects=True):
    field = pltpu.VMEM((nx, ny, nz), F32)
    found = [shift_scratch(ny, nz)] * 2 + [field]
    if injects:
        found += [pltpu.VMEM((2, SLOTS * 128, nz), BF16), field]
    return found


def clear_edges(ps_ref, qs_ref, ny):
    zero = jnp.zeros((ps_ref.shape[0], 8, 128), F32)
    for ref in (ps_ref, qs_ref):
        ref[:, 0:8, :] = zero
        ref[:, 8 + ny : 16 + ny, :] = zero


GROUP = 4


def first_local_kernel(
    p_far, k_far, b2_far, b3_far, out_far,
    p_ref, k_ref, b2_ref, b3_ref, out_ref, bands_ref, sems, *scratch,
):
    far = (p_far, k_far, b2_far, b3_far)
    near = (p_ref, k_ref, b2_ref, b3_ref)
    copies = [pltpu.make_async_copy(f, n, sems.at[i]) for i, (f, n) in enumerate(zip(far, near))]
    for copy in copies:
        copy.start()
    fill_bands(bands_ref)
    for copy in copies:
        copy.wait()
    local_change(p_ref, k_ref, b2_ref, b3_ref, bands_ref, None, None, 0, out_ref, scratch)
    store = pltpu.make_async_copy(out_ref, out_far, sems.at[4])
    store.start()
    store.wait()


def shift_scratch(ny, nz):
    return pltpu.VMEM((GROUP * (nz // 128), ny + 16, 128), F32)


def first_local(*arrays):
    nx, ny, nz = arrays[0].shape
    far = pl.BlockSpec(memory_space=pltpu.HBM)
    return pl.pallas_call(
        first_local_kernel,
        in_specs=[far] * 4,
        out_specs=far,
        out_shape=shape_of(nx, ny, nz),
        scratch_shapes=[pltpu.VMEM((nx, ny, nz), F32)] * 5
        + [pltpu.VMEM((4, nz, nz), BF16), pltpu.SemaphoreType.DMA((5,))]
        + local_scratch(nx, ny, nz, False),
        compiler_params=pltpu.CompilerParams(vmem_limit_bytes=16 * 1024 * 1024),
        name="first_local",
    )(*far_away(*arrays))


def first_inject_kernel(got_ref, local_far, *refs):
    count = (len(refs) - 6) // 2
    far, (out_ref, turned_ref, bands_ref), near = refs[:count], refs[count : count + 3], refs[count + 3 : -3]
    near_local_ref, spread_ref, sems = refs[-3:]
    first = pltpu.make_async_copy(local_far, near_local_ref, sems.at[0])
    first.start()
    copies = [pltpu.make_async_copy(f, n, sems.at[i + 1]) for i, (f, n) in enumerate(zip(far, near))]
    for copy in copies:
        copy.start()
    nx, ny, nz = out_ref.shape
    turned_ref[...] = got_ref[...].T
    fill_columns(got_ref, spread_ref, 0, nz)
    added = inject_rows(turned_ref[...], spread_ref, 0, nx * ny).reshape(nx, ny, nz)
    first.wait()
    out_ref[...] = near_local_ref[...] + added
    fill_bands(bands_ref)
    for copy in copies:
        copy.wait()


def first_inject(got, nearby, *arrays):
    nx, ny, nz = nearby.shape
    vmem = pl.BlockSpec(memory_space=pltpu.VMEM)
    far = pl.BlockSpec(memory_space=pltpu.HBM)
    return pl.pallas_call(
        first_inject_kernel,
        in_specs=[vmem] + [far] * (1 + len(arrays)),
        out_specs=[vmem] * (3 + len(arrays)),
        out_shape=[shape_of(nx, ny, nz), shape_of(128, 128), shape_of(4, nz, nz, dtype=BF16)]
        + [shape_of(*a.shape, dtype=a.dtype) for a in arrays],
        scratch_shapes=[
            pltpu.VMEM((nx, ny, nz), F32),
            pltpu.VMEM((2, SLOTS * 128, nz), BF16),
            pltpu.SemaphoreType.DMA((1 + len(arrays),)),
        ],
        compiler_params=PARAMS,
        name="first_inject",
    )(got, *far_away(nearby, *arrays))


def make_local_kernel(moment):
    def local_kernel(*refs):
        p_ref, bands_ref, k_ref, b2_ref, b3_ref, f_ref, change_ref = refs[:7]
        refs = refs[7:]
        if moment > 1:
            image_ref, refs = refs[0], refs[1:]
            light_ref, refs = refs[0], refs[1:]
        got_ref, turned_ref, out_ref, image_out_ref, light_out_ref, *scratch = refs

        def accumulate(x):
            frame = f_ref[moment - 1, x].astype(F32)
            image = frame * change_ref[x]
            light = frame * frame
            if moment > 1:
                image = image + image_ref[x]
                light = light + light_ref[x]
            if moment == f_ref.shape[0] - 1:
                frame = f_ref[moment, x].astype(F32)
                light = light + frame * frame
            image_out_ref[x] = image
            light_out_ref[x] = light

        local_change(
            p_ref, k_ref, b2_ref, b3_ref, bands_ref, got_ref, turned_ref[...], moment, out_ref,
            scratch, accumulate,
        )

    return local_kernel


def local_step(moment, current, bands, stiffness, b2, b3, frames, change, sums, got, turned):
    nx, ny, nz = current.shape
    images = list(sums) if moment > 1 else []
    return pl.pallas_call(
        make_local_kernel(moment),
        in_specs=[pl.BlockSpec(memory_space=pltpu.VMEM)] * (9 + len(images)),
        out_specs=[pl.BlockSpec(memory_space=pltpu.VMEM)] * 3,
        out_shape=[shape_of(nx, ny, nz)] * 3,
        scratch_shapes=local_scratch(nx, ny, nz),
        compiler_params=PARAMS,
        name="local_step",
    )(current, bands, stiffness, b2, b3, frames, change, *images, got, turned)


def edge_factors(place_ref, nx):
    first = place_ref[3]
    return (
        jnp.where(first > 0, 1.0, 0.0).astype(F32),
        jnp.where(first < place_ref[4], 1.0, 0.0).astype(F32),
    )


def change_column(edges, p_refs, b_refs, k_ref, local_ref, rows, lanes):
    pl_ref, pm_ref, pr_ref = p_refs
    bl_ref, bm_ref, br_ref = b_refs
    nx = pm_ref.shape[0]

    def cell(i):
        if i < 0:
            return edges[0] * pl_ref[HALO + i, rows, lanes]
        if i >= nx:
            return edges[1] * pr_ref[i - nx, rows, lanes]
        return pm_ref[i, rows, lanes]

    def face(i):
        if i < 0:
            return edges[0] * bl_ref[HALO + 4 + i, rows, lanes]
        if i >= nx:
            return edges[1] * br_ref[HALO + i - nx, rows, lanes]
        return bm_ref[i, rows, lanes]

    cells = {i: cell(i) for i in range(-HALO, 0)}
    fluxes = {}
    for ahead in range(0, nx + HALO):
        cells[ahead] = cell(ahead)
        j = ahead - 4
        if j >= -4:
            fluxes[j] = face(j) * weighted([(cells[j + k], cells[j + 1 - k]) for k in range(1, 5)])
        i = j - 3
        if i >= 0:
            total = weighted([(fluxes[i + k - 1], fluxes[i - k]) for k in range(1, 5)])
            yield i, cells[i], local_ref[i, rows, lanes] + k_ref[i, rows, lanes] * total


def each_column(ny, nz, work):
    def band(index, carry):
        for c in range(nz // 128):
            work(pl.ds(pl.multiple_of(index * 8, 8), 8), slice(c * 128, c * 128 + 128), index, c)
        return carry

    lax.fori_loop(0, ny // 8, band, 0)


def update_kernel(
    place_ref, pl_ref, pm_ref, pr_ref, bl_ref, bm_ref, br_ref, k_ref, local_ref, before_ref,
    next_ref, change_ref, head_ref, tail_ref,
):
    nx, ny, nz = pm_ref.shape
    edges = edge_factors(place_ref, nx)

    def work(rows, lanes, band, tile):
        for i, now, change in change_column(
            edges, (pl_ref, pm_ref, pr_ref), (bl_ref, bm_ref, br_ref), k_ref, local_ref, rows, lanes
        ):
            following = 2.0 * now - before_ref[i, rows, lanes] + change
            next_ref[i, rows, lanes] = following
            change_ref[i, rows, lanes] = change
            if i < HALO:
                head_ref[i, rows, lanes] = following
            if i >= nx - HALO:
                tail_ref[i - (nx - HALO), rows, lanes] = following

    each_column(ny, nz, work)


def last_kernel(
    place_ref, pl_ref, pm_ref, pr_ref, bl_ref, bm_ref, br_ref, k_ref, local_ref,
    before_ref, image_ref, f_ref, light_ref, now_far, next_ref, muted_ref, kept_ref, sem,
):
    nx, ny, nz = pm_ref.shape
    store = pltpu.make_async_copy(pm_ref, now_far, sem)
    store.start()
    steps = f_ref.shape[0]
    edges = edge_factors(place_ref, nx)
    second = lax.broadcasted_iota(jnp.int32, (8, 128), 0).astype(F32)
    third = lax.broadcasted_iota(jnp.int32, (8, 128), 1).astype(F32)
    first_at = (place_ref[3] - place_ref[0]).astype(F32)
    second_at = place_ref[1].astype(F32)
    third_at = place_ref[2].astype(F32)

    def work(rows, lanes, band, tile):
        flat = (second + ((band * 8).astype(F32) - second_at)) ** 2 + (
            third + (float(tile * 128) - third_at)
        ) ** 2
        for i, now, change in change_column(
            edges, (pl_ref, pm_ref, pr_ref), (bl_ref, bm_ref, br_ref), k_ref, local_ref, rows, lanes
        ):
            next_ref[i, rows, lanes] = 2.0 * now - before_ref[i, rows, lanes] + change
            image = image_ref[i, rows, lanes] + f_ref[steps - 1, i, rows, lanes].astype(F32) * change
            distance = (first_at + float(i)) ** 2 + flat
            kept_ref[i, rows, lanes] = (1.0 - jnp.exp(distance * (-1.0 / (2.0 * MUTE * MUTE)))) * image

    each_column(ny, nz, work)
    for y in range(ny):
        muted_ref[y // 2, y % 2, :, :] = kept_ref[:, y, :]
        muted_ref[y // 2, 2 + y % 2, :, :] = light_ref[:, y, :]
    store.wait()


def update_step(place, halos, current, b1_halos, b1, stiffness, local, before):
    nx, ny, nz = current.shape
    return pl.pallas_call(
        update_kernel,
        in_specs=[pl.BlockSpec(memory_space=pltpu.SMEM)] + [pl.BlockSpec(memory_space=pltpu.VMEM)] * 9,
        out_specs=[pl.BlockSpec(memory_space=pltpu.VMEM)] * 4,
        out_shape=[shape_of(nx, ny, nz)] * 2 + [shape_of(HALO, ny, nz)] * 2,
        compiler_params=PARAMS,
        name="update_step",
    )(place, halos[0], current, halos[1], b1_halos[0], b1, b1_halos[1], stiffness, local, before)


def last_step(place, halos, current, b1_halos, b1, stiffness, local, before, image, forward, light):
    nx, ny, nz = current.shape
    vmem = pl.BlockSpec(memory_space=pltpu.VMEM)
    smem = pl.BlockSpec(memory_space=pltpu.SMEM)
    return pl.pallas_call(
        last_kernel,
        in_specs=[smem] + [vmem] * 12,
        out_specs=[pl.BlockSpec(memory_space=pltpu.HBM)] + [vmem] * 2,
        out_shape=[shape_of(nx, ny, nz)] * 2 + [shape_of(ny // 2, 4, nx, nz)],
        scratch_shapes=[pltpu.VMEM((nx, ny, nz), F32), pltpu.SemaphoreType.DMA],
        compiler_params=PARAMS,
        name="last_step",
    )(
        place, halos[0], current, halos[1], b1_halos[0], b1, b1_halos[1], stiffness, local,
        before, image, forward, light,
    )


def quotient_kernel(image_ref, out_ref, *, scale):
    nz = image_ref.shape[-1]
    for side in range(2):
        image = image_ref[0, side]
        light = image_ref[0, 2 + side]
        for shot in range(1, image_ref.shape[0]):
            image = image + image_ref[shot, side]
            light = light + image_ref[shot, 2 + side]
        out_ref[:, side * nz : (side + 1) * nz] = image / (light * scale + DAMP)


def quotient(images, scale):
    _, _, nx, nz = images.shape
    return pl.pallas_call(
        lambda *refs: quotient_kernel(*refs, scale=scale),
        out_shape=shape_of(nx, 2 * nz),
        compiler_params=PARAMS,
        name="quotient",
    )(images)


def exchange(head, tail):
    count = lax.axis_size("sub")
    from_left = lax.ppermute(tail, "sub", [(i, (i + 1) % count) for i in range(count)])
    from_right = lax.ppermute(head, "sub", [((i + 1) % count, i) for i in range(count)])
    return from_left, from_right


def local(
    stiffness, b1, b2, b3, adjoint_before, adjoint_current, forward_field,
    traces, receiver_target, receiver_cell, source_cell,
):
    both = ("shot", "sub")
    steps = forward_field.shape[1]
    nx = stiffness.shape[0]
    rows = traces.shape[0]
    forward = forward_field[0]
    before = adjoint_before[0]
    current = adjoint_current[0]

    nx_all = nx * lax.axis_size("sub")
    place = jnp.concatenate(
        [
            source_cell[0],
            (lax.axis_index("sub") * nx).astype(jnp.int32)[None],
            jnp.full((1,), nx_all - nx, jnp.int32),
        ]
    )
    send, right, left = prep(
        traces, receiver_target.reshape(1, rows), receiver_cell.reshape(1, rows), current, b1
    )
    got = lax.all_to_all(send, both, split_axis=0, concat_axis=0, tiled=True)
    halos = exchange(left, right)
    b1_halos = halos
    nearby = first_local(current, stiffness, b2, b3)
    got, place = lax.optimization_barrier((got, place))
    nearby, turned, bands, current, stiffness, b2, b3, b1, before, frames = first_inject(
        got, nearby, current, stiffness, b2, b3, b1, before, forward
    )

    image = light = None
    for moment in range(steps - 1):
        following, change, head, tail = update_step(
            place, halos, current, b1_halos, b1, stiffness, nearby, before
        )
        halos = exchange(head, tail)
        before, current = current, following
        nearby, image, light = local_step(
            moment + 1, current, bands, stiffness, b2, b3, frames, change, (image, light), got, turned
        )
    now, following, sums = last_step(
        place, halos, current, b1_halos, b1, stiffness, nearby, before, image, frames, light
    )
    sums = lax.all_to_all(sums, "shot", split_axis=0, concat_axis=0, tiled=True)
    gradient = quotient(sums, 1.0 / (steps * lax.axis_size("shot")))
    return gradient, now[None], following[None]


def solution(mesh):
    placed = (
        P("sub", None, None),
        P("sub", None, None),
        P("sub", None, None),
        P("sub", None, None),
        P("shot", "sub", None, None),
        P("shot", "sub", None, None),
        P("shot", None, "sub", None, None),
        P(("shot", "sub"), None),
        P(("shot", "sub"), None),
        P(("shot", "sub")),
        P("shot", None),
    )
    return jax.shard_map(
        local,
        mesh=mesh,
        in_specs=placed,
        out_specs=(P("sub", "shot"), P("shot", "sub", None, None), P("shot", "sub", None, None)),
        check_vma=False,
    )
```

```python
import jax
import jax.numpy as jnp
import numpy as np
from jax import lax
from jax.experimental import pallas as pl
from jax.experimental.pallas import tpu as pltpu
from jax.sharding import PartitionSpec as P

MUTE = 6
COEFFS = (1225.0 / 1024.0, -245.0 / 3072.0, 49.0 / 5120.0, -5.0 / 7168.0)
DAMP = 0.1
HALO = 7
SLOTS = 6
FIELDS = 16
F32 = jnp.float32
BF16 = jnp.bfloat16
PARAMS = pltpu.CompilerParams(vmem_limit_bytes=8 * 1024 * 1024)


def shape_of(*dims, dtype=F32):
    return jax.ShapeDtypeStruct(dims, dtype)


def far_away(*arrays):
    return [pltpu.with_memory_space_constraint(a, pltpu.HBM) for a in arrays]


def split2(x):
    high = x.astype(BF16)
    return high, (x - high.astype(F32)).astype(BF16)


def split3(x):
    high = x.astype(BF16)
    rest = x - high.astype(F32)
    mid = rest.astype(BF16)
    return high, mid, (rest - mid.astype(F32)).astype(BF16)


def contract_last(left, right, **kwargs):
    return lax.dot_general(
        left, right, (((1,), (1,)), ((), ())), preferred_element_type=F32, **kwargs
    )


def prep_kernel(
    traces_far, kernel_far, target_far, cell_far, p_ref, b_ref,
    send_ref, right_ref, left_ref, traces_ref, kernel_ref, target_ref, cell_ref, sems, *, nz,
):
    nx = p_ref.shape[0]
    loads = [
        pltpu.make_async_copy(traces_far, traces_ref, sems.at[0]),
        pltpu.make_async_copy(kernel_far, kernel_ref, sems.at[1]),
        pltpu.make_async_copy(target_far, target_ref, sems.at[2]),
        pltpu.make_async_copy(cell_far, cell_ref, sems.at[3]),
    ]
    copies = [
        pltpu.make_async_copy(p_ref.at[pl.ds(nx - HALO, HALO)], right_ref.at[pl.ds(0, HALO)], sems.at[4]),
        pltpu.make_async_copy(b_ref.at[pl.ds(nx - 4, 4)], right_ref.at[pl.ds(HALO, 4)], sems.at[5]),
        pltpu.make_async_copy(p_ref.at[pl.ds(0, HALO)], left_ref.at[pl.ds(0, HALO)], sems.at[6]),
        pltpu.make_async_copy(b_ref.at[pl.ds(0, 3)], left_ref.at[pl.ds(HALO, 3)], sems.at[7]),
    ]
    for copy in loads + copies:
        copy.start()
    for load in loads:
        load.wait()
    rows = traces_ref.shape[0]
    values = contract_last(kernel_ref[...], traces_ref[...], precision=lax.Precision.HIGHEST)
    lane = lax.broadcasted_iota(jnp.int32, (128, rows), 0)
    hit = target_ref[...] == lane
    onehot = jnp.where(hit, 1.0, 0.0)
    upper = (
        lax.broadcasted_iota(jnp.int32, (rows, rows), 0)
        <= lax.broadcasted_iota(jnp.int32, (rows, rows), 1)
    )
    running = jnp.dot(
        onehot.astype(BF16),
        jnp.where(upper, 1.0, 0.0).astype(BF16),
        preferred_element_type=F32,
    )
    slot = (jnp.sum(jnp.where(hit, running, 0.0), axis=0, keepdims=True) - 1.0).astype(jnp.int32)
    cell = cell_ref[...]
    entries = jnp.where(lane % FIELDS == 8, (cell // nz).astype(F32), values)
    entries = jnp.where(lane % FIELDS == 9, (cell % nz).astype(F32), entries)
    entries = jnp.where(lane // FIELDS == slot, entries, 0.0)
    packed = jnp.zeros((128, 128), F32)
    for piece in split3(entries):
        packed = packed + contract_last(onehot.astype(BF16), piece)
    send_ref[...] = packed
    for copy in copies:
        copy.wait()


def prep(traces, target, cell, current, b1):
    nx, ny, nz = current.shape
    samples = traces.shape[1]
    position = np.arange(samples, dtype=np.float32)[None, :]
    centers = (np.arange(8, dtype=np.float32)[:, None] + np.float32(0.5)) * np.float32(samples / 8)
    kernel = (0.25 * np.exp(-np.abs(position - centers) / np.float32(samples / 8.0))).astype(np.float32)
    tiled = np.zeros((128, samples), np.float32)
    for slot in range(SLOTS):
        tiled[slot * FIELDS : slot * FIELDS + 8] = kernel
    vmem = pl.BlockSpec(memory_space=pltpu.VMEM)
    far = pl.BlockSpec(memory_space=pltpu.HBM)
    return pl.pallas_call(
        lambda *refs: prep_kernel(*refs, nz=nz),
        in_specs=[far] * 6,
        out_specs=[vmem] * 3,
        out_shape=[shape_of(128, 128), shape_of(HALO + 4, ny, nz), shape_of(HALO + 3, ny, nz)],
        scratch_shapes=[
            pltpu.VMEM(traces.shape, F32),
            pltpu.VMEM((128, samples), F32),
            pltpu.VMEM(target.shape, jnp.int32),
            pltpu.VMEM(cell.shape, jnp.int32),
            pltpu.SemaphoreType.DMA((8,)),
        ],
        compiler_params=PARAMS,
        name="prep",
    )(*far_away(traces, jnp.asarray(tiled), target, cell, current, b1))


def fill_columns(got_ref, spread_ref, moment, nz):
    zlane = lax.broadcasted_iota(jnp.int32, (128, nz), 1)
    for slot in range(SLOTS):
        base = slot * FIELDS
        third = got_ref[:, base + 9 : base + 10].astype(jnp.int32)
        value = got_ref[:, base + moment : base + moment + 1]
        spread = jnp.where(third == zlane, value, 0.0)
        high, low = split2(spread)
        spread_ref[0, slot * 128 : (slot + 1) * 128, :] = high
        spread_ref[1, slot * 128 : (slot + 1) * 128, :] = low


def inject_rows(turned, spread_ref, first_row, count):
    row = first_row + lax.broadcasted_iota(jnp.int32, (count, 128), 0)
    picks = []
    for slot in range(SLOTS):
        base = slot * FIELDS
        line = turned[base + 8 : base + 9, :].astype(jnp.int32)
        picks.append(jnp.where(line == row, 1.0, 0.0).astype(BF16))
    pick = jnp.concatenate(picks, axis=1)
    return jnp.dot(pick, spread_ref[0], preferred_element_type=F32) + jnp.dot(
        pick, spread_ref[1], preferred_element_type=F32
    )


def weighted(pairs):
    total = None
    for k, (ahead, behind) in enumerate(pairs):
        term = COEFFS[k] * (ahead - behind)
        total = term if total is None else total + term
    return total


def fill_bands(bands_ref):
    nz = bands_ref.shape[1]
    gap = lax.broadcasted_iota(jnp.int32, (nz, nz), 0) - lax.broadcasted_iota(
        jnp.int32, (nz, nz), 1
    )
    for side in range(2):
        band = jnp.zeros((nz, nz), F32)
        for k in range(1, 5):
            band = jnp.where(gap == k - side, COEFFS[k - 1], band)
            band = jnp.where(gap == 1 - k - side, -COEFFS[k - 1], band)
        high, low = split2(band)
        bands_ref[2 * side] = high
        bands_ref[2 * side + 1] = low


def banded(value, bands_ref, first):
    high, low = split2(value)
    return (
        jnp.dot(high, bands_ref[first], preferred_element_type=F32)
        + jnp.dot(low, bands_ref[first], preferred_element_type=F32)
        + jnp.dot(high, bands_ref[first + 1], preferred_element_type=F32)
    )


def second_derivative(ref, where, first, ny):
    return weighted(
        [
            (
                ref[where, 7 + first + k : 7 + first + k + ny, :],
                ref[where, 8 + first - k : 8 + first - k + ny, :],
            )
            for k in range(1, 5)
        ]
    )


def along_third(p_ref, b3_ref, bands_ref):
    nx, ny, nz = p_ref.shape
    flux = b3_ref[...].reshape(nx * ny, nz) * banded(p_ref[...].reshape(nx * ny, nz), bands_ref, 0)
    return banded(flux, bands_ref, 2)


def along_second(p_ref, b2_ref, x, lanes, ps_ref, qs_ref, where):
    ny = p_ref.shape[1]
    ps_ref[where, 8 : 8 + ny, :] = p_ref[x, :, lanes]
    qs_ref[where, 8 : 8 + ny, :] = b2_ref[x, :, lanes] * second_derivative(ps_ref, where, 1, ny)
    return second_derivative(qs_ref, where, 0, ny)


def local_change(
    p_ref, k_ref, b2_ref, b3_ref, bands_ref, got_ref, turned, moment, out_ref, scratch, and_then=None,
    loads=(),
):
    ps_ref, qs_ref, third_ref, *more = scratch
    nx, ny, nz = p_ref.shape
    clear_edges(ps_ref, qs_ref, ny)
    if got_ref is not None:
        spread_ref, added_ref = more
        fill_columns(got_ref, spread_ref, moment, nz)
        added_ref[...] = inject_rows(turned, spread_ref, 0, nx * ny).reshape(nx, ny, nz)
    for load in loads[:1]:
        load.wait()
    third_ref[...] = along_third(p_ref, b3_ref, bands_ref).reshape(nx, ny, nz)
    count = nz // 128
    for load in loads[1:]:
        load.wait()

    def planes(group, carry):
        for index in range(GROUP):
            x = group * GROUP + index
            for c in range(count):
                lanes = slice(c * 128, c * 128 + 128)
                second = along_second(p_ref, b2_ref, x, lanes, ps_ref, qs_ref, index * count + c)
                value = k_ref[x, :, lanes] * (second + third_ref[x, :, lanes])
                if got_ref is not None:
                    value = value + added_ref[x, :, lanes]
                out_ref[x, :, lanes] = value
            if and_then is not None:
                and_then(x)
        return carry

    lax.fori_loop(0, nx // GROUP, planes, 0)


def local_scratch(nx, ny, nz, injects=True):
    field = pltpu.VMEM((nx, ny, nz), F32)
    found = [shift_scratch(ny, nz)] * 2 + [field]
    if injects:
        found += [pltpu.VMEM((2, SLOTS * 128, nz), BF16), field]
    return found


def clear_edges(ps_ref, qs_ref, ny):
    zero = jnp.zeros((ps_ref.shape[0], 8, 128), F32)
    for ref in (ps_ref, qs_ref):
        ref[:, 0:8, :] = zero
        ref[:, 8 + ny : 16 + ny, :] = zero


GROUP = 4


def first_local_kernel(
    p_far, k_far, b2_far, b3_far, out_far,
    p_ref, k_ref, b2_ref, b3_ref, out_ref, bands_ref, sems, *scratch,
):
    far = (p_far, k_far, b2_far, b3_far)
    near = (p_ref, k_ref, b2_ref, b3_ref)
    copies = [pltpu.make_async_copy(f, n, sems.at[i]) for i, (f, n) in enumerate(zip(far, near))]
    for copy in copies:
        copy.start()
    fill_bands(bands_ref)
    for copy in copies:
        copy.wait()
    local_change(p_ref, k_ref, b2_ref, b3_ref, bands_ref, None, None, 0, out_ref, scratch)
    store = pltpu.make_async_copy(out_ref, out_far, sems.at[4])
    store.start()
    store.wait()


def shift_scratch(ny, nz):
    return pltpu.VMEM((GROUP * (nz // 128), ny + 16, 128), F32)


def first_local(*arrays):
    nx, ny, nz = arrays[0].shape
    far = pl.BlockSpec(memory_space=pltpu.HBM)
    return pl.pallas_call(
        first_local_kernel,
        in_specs=[far] * 4,
        out_specs=far,
        out_shape=shape_of(nx, ny, nz),
        scratch_shapes=[pltpu.VMEM((nx, ny, nz), F32)] * 5
        + [pltpu.VMEM((4, nz, nz), BF16), pltpu.SemaphoreType.DMA((5,))]
        + local_scratch(nx, ny, nz, False),
        compiler_params=pltpu.CompilerParams(vmem_limit_bytes=16 * 1024 * 1024),
        name="first_local",
    )(*far_away(*arrays))


def first_inject_kernel(got_ref, local_far, *refs):
    count = (len(refs) - 6) // 2
    far, (out_ref, turned_ref, bands_ref), near = refs[:count], refs[count : count + 3], refs[count + 3 : -3]
    near_local_ref, spread_ref, sems = refs[-3:]
    first = pltpu.make_async_copy(local_far, near_local_ref, sems.at[0])
    first.start()
    copies = [pltpu.make_async_copy(f, n, sems.at[i + 1]) for i, (f, n) in enumerate(zip(far, near))]
    for copy in copies:
        copy.start()
    nx, ny, nz = out_ref.shape
    turned_ref[...] = got_ref[...].T
    fill_columns(got_ref, spread_ref, 0, nz)
    added = inject_rows(turned_ref[...], spread_ref, 0, nx * ny).reshape(nx, ny, nz)
    first.wait()
    out_ref[...] = near_local_ref[...] + added
    fill_bands(bands_ref)
    for copy in copies:
        copy.wait()


def first_inject(got, nearby, *arrays):
    nx, ny, nz = nearby.shape
    vmem = pl.BlockSpec(memory_space=pltpu.VMEM)
    far = pl.BlockSpec(memory_space=pltpu.HBM)
    return pl.pallas_call(
        first_inject_kernel,
        in_specs=[vmem] + [far] * (1 + len(arrays)),
        out_specs=[vmem] * (3 + len(arrays)),
        out_shape=[shape_of(nx, ny, nz), shape_of(128, 128), shape_of(4, nz, nz, dtype=BF16)]
        + [shape_of(*a.shape, dtype=a.dtype) for a in arrays],
        scratch_shapes=[
            pltpu.VMEM((nx, ny, nz), F32),
            pltpu.VMEM((2, SLOTS * 128, nz), BF16),
            pltpu.SemaphoreType.DMA((1 + len(arrays),)),
        ],
        compiler_params=PARAMS,
        name="first_inject",
    )(got, *far_away(nearby, *arrays))


def make_local_kernel(moment):
    def local_kernel(*refs):
        p_ref, bands_ref, k_ref, b2_ref, b3_ref, f_ref, change_ref = refs[:7]
        refs = refs[7:]
        if moment > 1:
            image_ref, refs = refs[0], refs[1:]
            light_ref, refs = refs[0], refs[1:]
        got_ref, turned_ref, out_ref, image_out_ref, light_out_ref, *scratch = refs
        loads = ()
        if moment == 1:
            far = (b3_ref, b2_ref, f_ref)
            b3_ref, b2_ref, f_ref, *scratch, sems = scratch
            near = (b3_ref, b2_ref, f_ref)
            loads = [pltpu.make_async_copy(f, n, sems.at[i]) for i, (f, n) in enumerate(zip(far, near))]
            for load in loads:
                load.start()

        def accumulate(x):
            frame = f_ref[moment - 1, x].astype(F32)
            image = frame * change_ref[x]
            light = frame * frame
            if moment > 1:
                image = image + image_ref[x]
                light = light + light_ref[x]
            if moment == f_ref.shape[0] - 1:
                frame = f_ref[moment, x].astype(F32)
                light = light + frame * frame
            image_out_ref[x] = image
            light_out_ref[x] = light

        local_change(
            p_ref, k_ref, b2_ref, b3_ref, bands_ref, got_ref, turned_ref[...], moment, out_ref,
            scratch, accumulate, loads,
        )

    return local_kernel


def local_step(moment, current, bands, stiffness, b2, b3, frames, change, sums, got, turned):
    nx, ny, nz = current.shape
    vmem = pl.BlockSpec(memory_space=pltpu.VMEM)
    images, wide, moved, sems = list(sums), [vmem] * 3, [], []
    if moment == 1:
        images, wide = [], [pl.BlockSpec(memory_space=pltpu.HBM)] * 3
        moved = [shape_of(*a.shape, dtype=a.dtype) for a in (b3, b2, frames)]
        sems = [pltpu.SemaphoreType.DMA((3,))]
        b2, b3, frames = far_away(b2, b3, frames)
    return pl.pallas_call(
        make_local_kernel(moment),
        in_specs=[vmem] * 3 + wide + [vmem] * (3 + len(images)),
        out_specs=[vmem] * (3 + len(moved)),
        out_shape=[shape_of(nx, ny, nz)] * 3 + moved,
        scratch_shapes=local_scratch(nx, ny, nz) + sems,
        compiler_params=PARAMS,
        name="local_step",
    )(current, bands, stiffness, b2, b3, frames, change, *images, got, turned)


def edge_factors(place_ref, nx):
    first = place_ref[3]
    return (
        jnp.where(first > 0, 1.0, 0.0).astype(F32),
        jnp.where(first < place_ref[4], 1.0, 0.0).astype(F32),
    )


def change_column(edges, p_refs, b_refs, k_ref, local_ref, rows, lanes):
    pl_ref, pm_ref, pr_ref = p_refs
    bl_ref, bm_ref, br_ref = b_refs
    nx = pm_ref.shape[0]

    def cell(i):
        if i < 0:
            return edges[0] * pl_ref[HALO + i, rows, lanes]
        if i >= nx:
            return edges[1] * pr_ref[i - nx, rows, lanes]
        return pm_ref[i, rows, lanes]

    def face(i):
        if i < 0:
            return edges[0] * bl_ref[HALO + 4 + i, rows, lanes]
        if i >= nx:
            return edges[1] * br_ref[HALO + i - nx, rows, lanes]
        return bm_ref[i, rows, lanes]

    cells = {i: cell(i) for i in range(-HALO, 0)}
    fluxes = {}
    for ahead in range(0, nx + HALO):
        cells[ahead] = cell(ahead)
        j = ahead - 4
        if j >= -4:
            fluxes[j] = face(j) * weighted([(cells[j + k], cells[j + 1 - k]) for k in range(1, 5)])
        i = j - 3
        if i >= 0:
            total = weighted([(fluxes[i + k - 1], fluxes[i - k]) for k in range(1, 5)])
            yield i, cells[i], local_ref[i, rows, lanes] + k_ref[i, rows, lanes] * total


def each_column(ny, nz, work):
    def band(index, carry):
        for c in range(nz // 128):
            work(pl.ds(pl.multiple_of(index * 8, 8), 8), slice(c * 128, c * 128 + 128), index, c)
        return carry

    lax.fori_loop(0, ny // 8, band, 0)


def update_kernel(
    place_ref, pl_ref, pm_ref, pr_ref, bl_ref, bm_ref, br_ref, k_ref, local_ref, before_ref,
    next_ref, change_ref, head_ref, tail_ref,
):
    nx, ny, nz = pm_ref.shape
    edges = edge_factors(place_ref, nx)

    def work(rows, lanes, band, tile):
        for i, now, change in change_column(
            edges, (pl_ref, pm_ref, pr_ref), (bl_ref, bm_ref, br_ref), k_ref, local_ref, rows, lanes
        ):
            following = 2.0 * now - before_ref[i, rows, lanes] + change
            next_ref[i, rows, lanes] = following
            change_ref[i, rows, lanes] = change
            if i < HALO:
                head_ref[i, rows, lanes] = following
            if i >= nx - HALO:
                tail_ref[i - (nx - HALO), rows, lanes] = following

    each_column(ny, nz, work)


def last_kernel(
    place_ref, pl_ref, pm_ref, pr_ref, bl_ref, bm_ref, br_ref, k_ref, local_ref,
    before_ref, image_ref, f_ref, light_ref, now_far, next_ref, muted_ref, kept_ref, sem,
):
    nx, ny, nz = pm_ref.shape
    store = pltpu.make_async_copy(pm_ref, now_far, sem)
    store.start()
    steps = f_ref.shape[0]
    edges = edge_factors(place_ref, nx)
    second = lax.broadcasted_iota(jnp.int32, (8, 128), 0).astype(F32)
    third = lax.broadcasted_iota(jnp.int32, (8, 128), 1).astype(F32)
    first_at = (place_ref[3] - place_ref[0]).astype(F32)
    second_at = place_ref[1].astype(F32)
    third_at = place_ref[2].astype(F32)

    def work(rows, lanes, band, tile):
        flat = (second + ((band * 8).astype(F32) - second_at)) ** 2 + (
            third + (float(tile * 128) - third_at)
        ) ** 2
        for i, now, change in change_column(
            edges, (pl_ref, pm_ref, pr_ref), (bl_ref, bm_ref, br_ref), k_ref, local_ref, rows, lanes
        ):
            next_ref[i, rows, lanes] = 2.0 * now - before_ref[i, rows, lanes] + change
            image = image_ref[i, rows, lanes] + f_ref[steps - 1, i, rows, lanes].astype(F32) * change
            distance = (first_at + float(i)) ** 2 + flat
            kept_ref[i, rows, lanes] = (1.0 - jnp.exp(distance * (-1.0 / (2.0 * MUTE * MUTE)))) * image

    each_column(ny, nz, work)
    for y in range(ny):
        muted_ref[y // 2, y % 2, :, :] = kept_ref[:, y, :]
        muted_ref[y // 2, 2 + y % 2, :, :] = light_ref[:, y, :]
    store.wait()


def update_step(place, halos, current, b1_halos, b1, stiffness, local, before):
    nx, ny, nz = current.shape
    return pl.pallas_call(
        update_kernel,
        in_specs=[pl.BlockSpec(memory_space=pltpu.SMEM)] + [pl.BlockSpec(memory_space=pltpu.VMEM)] * 9,
        out_specs=[pl.BlockSpec(memory_space=pltpu.VMEM)] * 4,
        out_shape=[shape_of(nx, ny, nz)] * 2 + [shape_of(HALO, ny, nz)] * 2,
        compiler_params=PARAMS,
        name="update_step",
    )(place, halos[0], current, halos[1], b1_halos[0], b1, b1_halos[1], stiffness, local, before)


def last_step(place, halos, current, b1_halos, b1, stiffness, local, before, image, forward, light):
    nx, ny, nz = current.shape
    vmem = pl.BlockSpec(memory_space=pltpu.VMEM)
    smem = pl.BlockSpec(memory_space=pltpu.SMEM)
    return pl.pallas_call(
        last_kernel,
        in_specs=[smem] + [vmem] * 12,
        out_specs=[pl.BlockSpec(memory_space=pltpu.HBM)] + [vmem] * 2,
        out_shape=[shape_of(nx, ny, nz)] * 2 + [shape_of(ny // 2, 4, nx, nz)],
        scratch_shapes=[pltpu.VMEM((nx, ny, nz), F32), pltpu.SemaphoreType.DMA],
        compiler_params=PARAMS,
        name="last_step",
    )(
        place, halos[0], current, halos[1], b1_halos[0], b1, b1_halos[1], stiffness, local,
        before, image, forward, light,
    )


def quotient_kernel(image_ref, out_ref, *, scale):
    nz = image_ref.shape[-1]
    for side in range(2):
        image = image_ref[0, side]
        light = image_ref[0, 2 + side]
        for shot in range(1, image_ref.shape[0]):
            image = image + image_ref[shot, side]
            light = light + image_ref[shot, 2 + side]
        out_ref[:, side * nz : (side + 1) * nz] = image / (light * scale + DAMP)


def quotient(images, scale):
    _, _, nx, nz = images.shape
    return pl.pallas_call(
        lambda *refs: quotient_kernel(*refs, scale=scale),
        out_shape=shape_of(nx, 2 * nz),
        compiler_params=PARAMS,
        name="quotient",
    )(images)


def exchange(head, tail):
    count = lax.axis_size("sub")
    from_left = lax.ppermute(tail, "sub", [(i, (i + 1) % count) for i in range(count)])
    from_right = lax.ppermute(head, "sub", [((i + 1) % count, i) for i in range(count)])
    return from_left, from_right


def local(
    stiffness, b1, b2, b3, adjoint_before, adjoint_current, forward_field,
    traces, receiver_target, receiver_cell, source_cell,
):
    both = ("shot", "sub")
    steps = forward_field.shape[1]
    nx = stiffness.shape[0]
    rows = traces.shape[0]
    forward = forward_field[0]
    before = adjoint_before[0]
    current = adjoint_current[0]

    nx_all = nx * lax.axis_size("sub")
    place = jnp.concatenate(
        [
            source_cell[0],
            (lax.axis_index("sub") * nx).astype(jnp.int32)[None],
            jnp.full((1,), nx_all - nx, jnp.int32),
        ]
    )
    send, right, left = prep(
        traces, receiver_target.reshape(1, rows), receiver_cell.reshape(1, rows), current, b1
    )
    got = lax.all_to_all(send, both, split_axis=0, concat_axis=0, tiled=True)
    halos = exchange(left, right)
    b1_halos = halos
    nearby = first_local(current, stiffness, b2, b3)
    got, place = lax.optimization_barrier((got, place))
    nearby, turned, bands, current, stiffness, b1, before = first_inject(
        got, nearby, current, stiffness, b1, before
    )
    frames = forward

    image = light = None
    for moment in range(steps - 1):
        following, change, head, tail = update_step(
            place, halos, current, b1_halos, b1, stiffness, nearby, before
        )
        halos = exchange(head, tail)
        before, current = current, following
        nearby, image, light, *moved = local_step(
            moment + 1, current, bands, stiffness, b2, b3, frames, change, (image, light), got, turned
        )
        if moved:
            b3, b2, frames = moved
    now, following, sums = last_step(
        place, halos, current, b1_halos, b1, stiffness, nearby, before, image, frames, light
    )
    sums = lax.all_to_all(sums, "shot", split_axis=0, concat_axis=0, tiled=True)
    gradient = quotient(sums, 1.0 / (steps * lax.axis_size("shot")))
    return gradient, now[None], following[None]


def solution(mesh):
    placed = (
        P("sub", None, None),
        P("sub", None, None),
        P("sub", None, None),
        P("sub", None, None),
        P("shot", "sub", None, None),
        P("shot", "sub", None, None),
        P("shot", None, "sub", None, None),
        P(("shot", "sub"), None),
        P(("shot", "sub"), None),
        P(("shot", "sub")),
        P("shot", None),
    )
    return jax.shard_map(
        local,
        mesh=mesh,
        in_specs=placed,
        out_specs=(P("sub", "shot"), P("shot", "sub", None, None), P("shot", "sub", None, None)),
        check_vma=False,
    )
```

```python
import jax
import jax.numpy as jnp
import numpy as np
from jax import lax
from jax.experimental import pallas as pl
from jax.experimental.pallas import tpu as pltpu
from jax.sharding import PartitionSpec as P

MUTE = 6
COEFFS = (1225.0 / 1024.0, -245.0 / 3072.0, 49.0 / 5120.0, -5.0 / 7168.0)
DAMP = 0.1
HALO = 7
SLOTS = 6
FIELDS = 16
F32 = jnp.float32
BF16 = jnp.bfloat16
PARAMS = pltpu.CompilerParams(vmem_limit_bytes=8 * 1024 * 1024)


def shape_of(*dims, dtype=F32):
    return jax.ShapeDtypeStruct(dims, dtype)


def far_away(*arrays):
    return [pltpu.with_memory_space_constraint(a, pltpu.HBM) for a in arrays]


def split2(x):
    high = x.astype(BF16)
    return high, (x - high.astype(F32)).astype(BF16)


def split3(x):
    high = x.astype(BF16)
    rest = x - high.astype(F32)
    mid = rest.astype(BF16)
    return high, mid, (rest - mid.astype(F32)).astype(BF16)


def contract_last(left, right, **kwargs):
    return lax.dot_general(
        left, right, (((1,), (1,)), ((), ())), preferred_element_type=F32, **kwargs
    )


def prep_kernel(
    traces_far, kernel_far, target_far, cell_far, p_ref, b_ref,
    send_ref, right_ref, left_ref, traces_ref, kernel_ref, target_ref, cell_ref, sems, *, nz,
):
    nx = p_ref.shape[0]
    loads = [
        pltpu.make_async_copy(traces_far, traces_ref, sems.at[0]),
        pltpu.make_async_copy(kernel_far, kernel_ref, sems.at[1]),
        pltpu.make_async_copy(target_far, target_ref, sems.at[2]),
        pltpu.make_async_copy(cell_far, cell_ref, sems.at[3]),
    ]
    copies = [
        pltpu.make_async_copy(p_ref.at[pl.ds(nx - HALO, HALO)], right_ref.at[pl.ds(0, HALO)], sems.at[4]),
        pltpu.make_async_copy(b_ref.at[pl.ds(nx - 4, 4)], right_ref.at[pl.ds(HALO, 4)], sems.at[5]),
        pltpu.make_async_copy(p_ref.at[pl.ds(0, HALO)], left_ref.at[pl.ds(0, HALO)], sems.at[6]),
        pltpu.make_async_copy(b_ref.at[pl.ds(0, 3)], left_ref.at[pl.ds(HALO, 3)], sems.at[7]),
    ]
    for copy in loads + copies:
        copy.start()
    for load in loads:
        load.wait()
    rows = traces_ref.shape[0]
    values = contract_last(kernel_ref[...], traces_ref[...], precision=lax.Precision.HIGHEST)
    lane = lax.broadcasted_iota(jnp.int32, (128, rows), 0)
    hit = target_ref[...] == lane
    onehot = jnp.where(hit, 1.0, 0.0)
    upper = (
        lax.broadcasted_iota(jnp.int32, (rows, rows), 0)
        <= lax.broadcasted_iota(jnp.int32, (rows, rows), 1)
    )
    running = jnp.dot(
        onehot.astype(BF16),
        jnp.where(upper, 1.0, 0.0).astype(BF16),
        preferred_element_type=F32,
    )
    slot = (jnp.sum(jnp.where(hit, running, 0.0), axis=0, keepdims=True) - 1.0).astype(jnp.int32)
    cell = cell_ref[...]
    entries = jnp.where(lane % FIELDS == 8, (cell // nz).astype(F32), values)
    entries = jnp.where(lane % FIELDS == 9, (cell % nz).astype(F32), entries)
    entries = jnp.where(lane // FIELDS == slot, entries, 0.0)
    packed = jnp.zeros((128, 128), F32)
    for piece in split3(entries):
        packed = packed + contract_last(onehot.astype(BF16), piece)
    send_ref[...] = packed
    for copy in copies:
        copy.wait()


def prep(traces, target, cell, current, b1):
    nx, ny, nz = current.shape
    samples = traces.shape[1]
    position = np.arange(samples, dtype=np.float32)[None, :]
    centers = (np.arange(8, dtype=np.float32)[:, None] + np.float32(0.5)) * np.float32(samples / 8)
    kernel = (0.25 * np.exp(-np.abs(position - centers) / np.float32(samples / 8.0))).astype(np.float32)
    tiled = np.zeros((128, samples), np.float32)
    for slot in range(SLOTS):
        tiled[slot * FIELDS : slot * FIELDS + 8] = kernel
    vmem = pl.BlockSpec(memory_space=pltpu.VMEM)
    far = pl.BlockSpec(memory_space=pltpu.HBM)
    return pl.pallas_call(
        lambda *refs: prep_kernel(*refs, nz=nz),
        in_specs=[far] * 6,
        out_specs=[vmem] * 3,
        out_shape=[shape_of(128, 128), shape_of(HALO + 4, ny, nz), shape_of(HALO + 3, ny, nz)],
        scratch_shapes=[
            pltpu.VMEM(traces.shape, F32),
            pltpu.VMEM((128, samples), F32),
            pltpu.VMEM(target.shape, jnp.int32),
            pltpu.VMEM(cell.shape, jnp.int32),
            pltpu.SemaphoreType.DMA((8,)),
        ],
        compiler_params=PARAMS,
        name="prep",
    )(*far_away(traces, jnp.asarray(tiled), target, cell, current, b1))


def fill_columns(got_ref, spread_ref, moment, nz):
    zlane = lax.broadcasted_iota(jnp.int32, (128, nz), 1)
    for slot in range(SLOTS):
        base = slot * FIELDS
        third = got_ref[:, base + 9 : base + 10].astype(jnp.int32)
        value = got_ref[:, base + moment : base + moment + 1]
        spread = jnp.where(third == zlane, value, 0.0)
        high, low = split2(spread)
        spread_ref[0, slot * 128 : (slot + 1) * 128, :] = high
        spread_ref[1, slot * 128 : (slot + 1) * 128, :] = low


def inject_rows(turned, spread_ref, first_row, count):
    row = first_row + lax.broadcasted_iota(jnp.int32, (count, 128), 0)
    picks = []
    for slot in range(SLOTS):
        base = slot * FIELDS
        line = turned[base + 8 : base + 9, :].astype(jnp.int32)
        picks.append(jnp.where(line == row, 1.0, 0.0).astype(BF16))
    pick = jnp.concatenate(picks, axis=1)
    return jnp.dot(pick, spread_ref[0], preferred_element_type=F32) + jnp.dot(
        pick, spread_ref[1], preferred_element_type=F32
    )


def weighted(pairs):
    total = None
    for k, (ahead, behind) in enumerate(pairs):
        term = COEFFS[k] * (ahead - behind)
        total = term if total is None else total + term
    return total


def fill_bands(bands_ref):
    nz = bands_ref.shape[1]
    gap = lax.broadcasted_iota(jnp.int32, (nz, nz), 0) - lax.broadcasted_iota(
        jnp.int32, (nz, nz), 1
    )
    for side in range(2):
        band = jnp.zeros((nz, nz), F32)
        for k in range(1, 5):
            band = jnp.where(gap == k - side, COEFFS[k - 1], band)
            band = jnp.where(gap == 1 - k - side, -COEFFS[k - 1], band)
        high, low = split2(band)
        bands_ref[2 * side] = high
        bands_ref[2 * side + 1] = low


def banded(value, bands_ref, first):
    high, low = split2(value)
    return (
        jnp.dot(high, bands_ref[first], preferred_element_type=F32)
        + jnp.dot(low, bands_ref[first], preferred_element_type=F32)
        + jnp.dot(high, bands_ref[first + 1], preferred_element_type=F32)
    )


def second_derivative(ref, where, first, ny):
    return weighted(
        [
            (
                ref[where, 7 + first + k : 7 + first + k + ny, :],
                ref[where, 8 + first - k : 8 + first - k + ny, :],
            )
            for k in range(1, 5)
        ]
    )


def along_third(p_ref, b3_ref, bands_ref):
    nx, ny, nz = p_ref.shape
    flux = b3_ref[...].reshape(nx * ny, nz) * banded(p_ref[...].reshape(nx * ny, nz), bands_ref, 0)
    return banded(flux, bands_ref, 2)


def along_second(p_ref, b2_ref, x, lanes, ps_ref, qs_ref, where):
    ny = p_ref.shape[1]
    ps_ref[where, 8 : 8 + ny, :] = p_ref[x, :, lanes]
    qs_ref[where, 8 : 8 + ny, :] = b2_ref[x, :, lanes] * second_derivative(ps_ref, where, 1, ny)
    return second_derivative(qs_ref, where, 0, ny)


def local_change(
    p_ref, k_ref, b2_ref, b3_ref, bands_ref, got_ref, turned, moment, out_ref, scratch, and_then=None,
    loads=(),
):
    ps_ref, qs_ref, third_ref, *more = scratch
    nx, ny, nz = p_ref.shape
    clear_edges(ps_ref, qs_ref, ny)
    if got_ref is not None:
        spread_ref, added_ref = more
        fill_columns(got_ref, spread_ref, moment, nz)
        added_ref[...] = inject_rows(turned, spread_ref, 0, nx * ny).reshape(nx, ny, nz)
    for load in loads[:1]:
        load.wait()
    third_ref[...] = along_third(p_ref, b3_ref, bands_ref).reshape(nx, ny, nz)
    count = nz // 128
    for load in loads[1:]:
        load.wait()

    def planes(group, carry):
        for index in range(GROUP):
            x = group * GROUP + index
            for c in range(count):
                lanes = slice(c * 128, c * 128 + 128)
                second = along_second(p_ref, b2_ref, x, lanes, ps_ref, qs_ref, index * count + c)
                value = k_ref[x, :, lanes] * (second + third_ref[x, :, lanes])
                if got_ref is not None:
                    value = value + added_ref[x, :, lanes]
                out_ref[x, :, lanes] = value
            if and_then is not None:
                and_then(x)
        return carry

    lax.fori_loop(0, nx // GROUP, planes, 0)


def local_scratch(nx, ny, nz, injects=True):
    field = pltpu.VMEM((nx, ny, nz), F32)
    found = [shift_scratch(ny, nz)] * 2 + [field]
    if injects:
        found += [pltpu.VMEM((2, SLOTS * 128, nz), BF16), field]
    return found


def clear_edges(ps_ref, qs_ref, ny):
    zero = jnp.zeros((ps_ref.shape[0], 8, 128), F32)
    for ref in (ps_ref, qs_ref):
        ref[:, 0:8, :] = zero
        ref[:, 8 + ny : 16 + ny, :] = zero


GROUP = 4


def first_local_kernel(
    p_far, k_far, b2_far, b3_far, out_far,
    p_ref, k_ref, b2_ref, b3_ref, out_ref, bands_ref, sems, *scratch,
):
    far = (p_far, k_far, b2_far, b3_far)
    near = (p_ref, k_ref, b2_ref, b3_ref)
    copies = [pltpu.make_async_copy(f, n, sems.at[i]) for i, (f, n) in enumerate(zip(far, near))]
    for copy in copies:
        copy.start()
    fill_bands(bands_ref)
    for copy in copies:
        copy.wait()
    local_change(p_ref, k_ref, b2_ref, b3_ref, bands_ref, None, None, 0, out_ref, scratch)
    store = pltpu.make_async_copy(out_ref, out_far, sems.at[4])
    store.start()
    store.wait()


def shift_scratch(ny, nz):
    return pltpu.VMEM((GROUP * (nz // 128), ny + 16, 128), F32)


def first_local(*arrays):
    nx, ny, nz = arrays[0].shape
    far = pl.BlockSpec(memory_space=pltpu.HBM)
    return pl.pallas_call(
        first_local_kernel,
        in_specs=[far] * 4,
        out_specs=far,
        out_shape=shape_of(nx, ny, nz),
        scratch_shapes=[pltpu.VMEM((nx, ny, nz), F32)] * 5
        + [pltpu.VMEM((4, nz, nz), BF16), pltpu.SemaphoreType.DMA((5,))]
        + local_scratch(nx, ny, nz, False),
        compiler_params=pltpu.CompilerParams(vmem_limit_bytes=16 * 1024 * 1024),
        name="first_local",
    )(*far_away(*arrays))


def first_inject_kernel(got_ref, local_far, *refs):
    count = (len(refs) - 6) // 2
    far, (out_ref, turned_ref, bands_ref), near = refs[:count], refs[count : count + 3], refs[count + 3 : -3]
    near_local_ref, spread_ref, sems = refs[-3:]
    first = pltpu.make_async_copy(local_far, near_local_ref, sems.at[0])
    first.start()
    copies = [pltpu.make_async_copy(f, n, sems.at[i + 1]) for i, (f, n) in enumerate(zip(far, near))]
    for copy in copies:
        copy.start()
    nx, ny, nz = out_ref.shape
    turned_ref[...] = got_ref[...].T
    fill_columns(got_ref, spread_ref, 0, nz)
    added = inject_rows(turned_ref[...], spread_ref, 0, nx * ny).reshape(nx, ny, nz)
    first.wait()
    out_ref[...] = near_local_ref[...] + added
    fill_bands(bands_ref)
    for copy in copies:
        copy.wait()


def first_inject(got, nearby, *arrays):
    nx, ny, nz = nearby.shape
    vmem = pl.BlockSpec(memory_space=pltpu.VMEM)
    far = pl.BlockSpec(memory_space=pltpu.HBM)
    return pl.pallas_call(
        first_inject_kernel,
        in_specs=[vmem] + [far] * (1 + len(arrays)),
        out_specs=[vmem] * (3 + len(arrays)),
        out_shape=[shape_of(nx, ny, nz), shape_of(128, 128), shape_of(4, nz, nz, dtype=BF16)]
        + [shape_of(*a.shape, dtype=a.dtype) for a in arrays],
        scratch_shapes=[
            pltpu.VMEM((nx, ny, nz), F32),
            pltpu.VMEM((2, SLOTS * 128, nz), BF16),
            pltpu.SemaphoreType.DMA((1 + len(arrays),)),
        ],
        compiler_params=PARAMS,
        name="first_inject",
    )(got, *far_away(nearby, *arrays))


def make_local_kernel(moment):
    def local_kernel(*refs):
        p_ref, bands_ref, k_ref, b2_ref, b3_ref, f_ref, change_ref = refs[:7]
        refs = refs[7:]
        if moment > 1:
            image_ref, refs = refs[0], refs[1:]
            light_ref, refs = refs[0], refs[1:]
        got_ref, turned_ref, out_ref, image_out_ref, light_out_ref, *scratch = refs
        loads = ()
        if moment == 1:
            far = (b3_ref, b2_ref, f_ref)
            b3_ref, b2_ref, f_ref, *scratch, sems = scratch
            near = (b3_ref, b2_ref, f_ref)
            loads = [pltpu.make_async_copy(f, n, sems.at[i]) for i, (f, n) in enumerate(zip(far, near))]
            for load in loads:
                load.start()

        def accumulate(x):
            frame = f_ref[moment - 1, x].astype(F32)
            image = frame * change_ref[x]
            light = frame * frame
            if moment > 1:
                image = image + image_ref[x]
                light = light + light_ref[x]
            if moment == f_ref.shape[0] - 1:
                frame = f_ref[moment, x].astype(F32)
                light = light + frame * frame
            image_out_ref[x] = image
            light_out_ref[x] = light

        local_change(
            p_ref, k_ref, b2_ref, b3_ref, bands_ref, got_ref, turned_ref[...], moment, out_ref,
            scratch, accumulate, loads,
        )

    return local_kernel


def local_step(moment, current, bands, stiffness, b2, b3, frames, change, sums, got, turned):
    nx, ny, nz = current.shape
    vmem = pl.BlockSpec(memory_space=pltpu.VMEM)
    images, wide, moved, sems = list(sums), [vmem] * 3, [], []
    if moment == 1:
        images, wide = [], [pl.BlockSpec(memory_space=pltpu.HBM)] * 3
        moved = [shape_of(*a.shape, dtype=a.dtype) for a in (b3, b2, frames)]
        sems = [pltpu.SemaphoreType.DMA((3,))]
        b2, b3, frames = far_away(b2, b3, frames)
    return pl.pallas_call(
        make_local_kernel(moment),
        in_specs=[vmem] * 3 + wide + [vmem] * (3 + len(images)),
        out_specs=[vmem] * (3 + len(moved)),
        out_shape=[shape_of(nx, ny, nz)] * 3 + moved,
        scratch_shapes=local_scratch(nx, ny, nz) + sems,
        compiler_params=PARAMS,
        name="local_step",
    )(current, bands, stiffness, b2, b3, frames, change, *images, got, turned)


def edge_factors(place_ref, nx):
    first = place_ref[3]
    return (
        jnp.where(first > 0, 1.0, 0.0).astype(F32),
        jnp.where(first < place_ref[4], 1.0, 0.0).astype(F32),
    )


def change_column(edges, p_refs, b_refs, k_ref, local_ref, rows, lanes):
    pl_ref, pm_ref, pr_ref = p_refs
    bl_ref, bm_ref, br_ref = b_refs
    nx = pm_ref.shape[0]

    def cell(i):
        if i < 0:
            return edges[0] * pl_ref[HALO + i, rows, lanes]
        if i >= nx:
            return edges[1] * pr_ref[i - nx, rows, lanes]
        return pm_ref[i, rows, lanes]

    def face(i):
        if i < 0:
            return edges[0] * bl_ref[HALO + 4 + i, rows, lanes]
        if i >= nx:
            return edges[1] * br_ref[HALO + i - nx, rows, lanes]
        return bm_ref[i, rows, lanes]

    cells = {i: cell(i) for i in range(-HALO, 0)}
    fluxes = {}
    for ahead in range(0, nx + HALO):
        cells[ahead] = cell(ahead)
        j = ahead - 4
        if j >= -4:
            fluxes[j] = face(j) * weighted([(cells[j + k], cells[j + 1 - k]) for k in range(1, 5)])
        i = j - 3
        if i >= 0:
            total = weighted([(fluxes[i + k - 1], fluxes[i - k]) for k in range(1, 5)])
            yield i, cells[i], local_ref[i, rows, lanes] + k_ref[i, rows, lanes] * total


def each_column(ny, nz, work):
    def band(index, carry):
        for c in range(nz // 128):
            work(pl.ds(pl.multiple_of(index * 8, 8), 8), slice(c * 128, c * 128 + 128), index, c)
        return carry

    lax.fori_loop(0, ny // 8, band, 0)


def update_kernel(
    place_ref, pl_ref, pm_ref, pr_ref, bl_ref, bm_ref, br_ref, k_ref, local_ref, before_ref,
    next_ref, change_ref, head_ref, tail_ref,
):
    nx, ny, nz = pm_ref.shape
    edges = edge_factors(place_ref, nx)

    def work(rows, lanes, band, tile):
        for i, now, change in change_column(
            edges, (pl_ref, pm_ref, pr_ref), (bl_ref, bm_ref, br_ref), k_ref, local_ref, rows, lanes
        ):
            following = 2.0 * now - before_ref[i, rows, lanes] + change
            next_ref[i, rows, lanes] = following
            change_ref[i, rows, lanes] = change
            if i < HALO:
                head_ref[i, rows, lanes] = following
            if i >= nx - HALO:
                tail_ref[i - (nx - HALO), rows, lanes] = following

    each_column(ny, nz, work)


def last_kernel(
    place_ref, pl_ref, pm_ref, pr_ref, bl_ref, bm_ref, br_ref, k_ref, local_ref,
    before_ref, image_ref, f_ref, light_ref, now_far, next_far, sums_far,
    next_ref, muted_ref, kept_ref, sems,
):
    nx, ny, nz = pm_ref.shape
    store = pltpu.make_async_copy(pm_ref, now_far, sems.at[0])
    store.start()
    for y in range(ny):
        muted_ref[1, y // 2, y % 2, :, :] = light_ref[:, y, :]
    store_light = pltpu.make_async_copy(muted_ref.at[1], sums_far.at[:, pl.ds(2, 2)], sems.at[1])
    store_light.start()
    steps = f_ref.shape[0]
    edges = edge_factors(place_ref, nx)
    second = lax.broadcasted_iota(jnp.int32, (8, 128), 0).astype(F32)
    third = lax.broadcasted_iota(jnp.int32, (8, 128), 1).astype(F32)
    first_at = (place_ref[3] - place_ref[0]).astype(F32)
    second_at = place_ref[1].astype(F32)
    third_at = place_ref[2].astype(F32)

    def work(rows, lanes, band, tile):
        flat = (second + ((band * 8).astype(F32) - second_at)) ** 2 + (
            third + (float(tile * 128) - third_at)
        ) ** 2
        for i, now, change in change_column(
            edges, (pl_ref, pm_ref, pr_ref), (bl_ref, bm_ref, br_ref), k_ref, local_ref, rows, lanes
        ):
            next_ref[i, rows, lanes] = 2.0 * now - before_ref[i, rows, lanes] + change
            image = image_ref[i, rows, lanes] + f_ref[steps - 1, i, rows, lanes].astype(F32) * change
            distance = (first_at + float(i)) ** 2 + flat
            kept_ref[i, rows, lanes] = (1.0 - jnp.exp(distance * (-1.0 / (2.0 * MUTE * MUTE)))) * image

    each_column(ny, nz, work)
    store_next = pltpu.make_async_copy(next_ref, next_far, sems.at[2])
    store_next.start()
    for y in range(ny):
        muted_ref[0, y // 2, y % 2, :, :] = kept_ref[:, y, :]
    store_image = pltpu.make_async_copy(muted_ref.at[0], sums_far.at[:, pl.ds(0, 2)], sems.at[3])
    store_image.start()
    for copy in (store, store_light, store_next, store_image):
        copy.wait()


def update_step(place, halos, current, b1_halos, b1, stiffness, local, before):
    nx, ny, nz = current.shape
    return pl.pallas_call(
        update_kernel,
        in_specs=[pl.BlockSpec(memory_space=pltpu.SMEM)] + [pl.BlockSpec(memory_space=pltpu.VMEM)] * 9,
        out_specs=[pl.BlockSpec(memory_space=pltpu.VMEM)] * 4,
        out_shape=[shape_of(nx, ny, nz)] * 2 + [shape_of(HALO, ny, nz)] * 2,
        compiler_params=PARAMS,
        name="update_step",
    )(place, halos[0], current, halos[1], b1_halos[0], b1, b1_halos[1], stiffness, local, before)


def last_step(place, halos, current, b1_halos, b1, stiffness, local, before, image, forward, light):
    nx, ny, nz = current.shape
    vmem = pl.BlockSpec(memory_space=pltpu.VMEM)
    smem = pl.BlockSpec(memory_space=pltpu.SMEM)
    return pl.pallas_call(
        last_kernel,
        in_specs=[smem] + [vmem] * 12,
        out_specs=[pl.BlockSpec(memory_space=pltpu.HBM)] * 3,
        out_shape=[shape_of(nx, ny, nz)] * 2 + [shape_of(ny // 2, 4, nx, nz)],
        scratch_shapes=[
            pltpu.VMEM((nx, ny, nz), F32),
            pltpu.VMEM((2, ny // 2, 2, nx, nz), F32),
            pltpu.VMEM((nx, ny, nz), F32),
            pltpu.SemaphoreType.DMA((4,)),
        ],
        compiler_params=PARAMS,
        name="last_step",
    )(
        place, halos[0], current, halos[1], b1_halos[0], b1, b1_halos[1], stiffness, local,
        before, image, forward, light,
    )


def quotient_kernel(image_ref, out_ref, *, scale):
    nz = image_ref.shape[-1]
    for side in range(2):
        image = image_ref[0, side]
        light = image_ref[0, 2 + side]
        for shot in range(1, image_ref.shape[0]):
            image = image + image_ref[shot, side]
            light = light + image_ref[shot, 2 + side]
        out_ref[:, side * nz : (side + 1) * nz] = image / (light * scale + DAMP)


def quotient(images, scale):
    _, _, nx, nz = images.shape
    return pl.pallas_call(
        lambda *refs: quotient_kernel(*refs, scale=scale),
        out_shape=shape_of(nx, 2 * nz),
        compiler_params=PARAMS,
        name="quotient",
    )(images)


def exchange(head, tail):
    count = lax.axis_size("sub")
    from_left = lax.ppermute(tail, "sub", [(i, (i + 1) % count) for i in range(count)])
    from_right = lax.ppermute(head, "sub", [((i + 1) % count, i) for i in range(count)])
    return from_left, from_right


def local(
    stiffness, b1, b2, b3, adjoint_before, adjoint_current, forward_field,
    traces, receiver_target, receiver_cell, source_cell,
):
    both = ("shot", "sub")
    steps = forward_field.shape[1]
    nx = stiffness.shape[0]
    rows = traces.shape[0]
    forward = forward_field[0]
    before = adjoint_before[0]
    current = adjoint_current[0]

    nx_all = nx * lax.axis_size("sub")
    place = jnp.concatenate(
        [
            source_cell[0],
            (lax.axis_index("sub") * nx).astype(jnp.int32)[None],
            jnp.full((1,), nx_all - nx, jnp.int32),
        ]
    )
    send, right, left = prep(
        traces, receiver_target.reshape(1, rows), receiver_cell.reshape(1, rows), current, b1
    )
    got = lax.all_to_all(send, both, split_axis=0, concat_axis=0, tiled=True)
    halos = exchange(left, right)
    b1_halos = halos
    nearby = first_local(current, stiffness, b2, b3)
    got, place = lax.optimization_barrier((got, place))
    nearby, turned, bands, current, stiffness, b1, before = first_inject(
        got, nearby, current, stiffness, b1, before
    )
    frames = forward

    image = light = None
    for moment in range(steps - 1):
        following, change, head, tail = update_step(
            place, halos, current, b1_halos, b1, stiffness, nearby, before
        )
        halos = exchange(head, tail)
        before, current = current, following
        nearby, image, light, *moved = local_step(
            moment + 1, current, bands, stiffness, b2, b3, frames, change, (image, light), got, turned
        )
        if moved:
            b3, b2, frames = moved
    now, following, sums = last_step(
        place, halos, current, b1_halos, b1, stiffness, nearby, before, image, frames, light
    )
    sums = lax.all_to_all(sums, "shot", split_axis=0, concat_axis=0, tiled=True)
    gradient = quotient(sums, 1.0 / (steps * lax.axis_size("shot")))
    return gradient, now[None], following[None]


def solution(mesh):
    placed = (
        P("sub", None, None),
        P("sub", None, None),
        P("sub", None, None),
        P("sub", None, None),
        P("shot", "sub", None, None),
        P("shot", "sub", None, None),
        P("shot", None, "sub", None, None),
        P(("shot", "sub"), None),
        P(("shot", "sub"), None),
        P(("shot", "sub")),
        P("shot", None),
    )
    return jax.shard_map(
        local,
        mesh=mesh,
        in_specs=placed,
        out_specs=(P("sub", "shot"), P("shot", "sub", None, None), P("shot", "sub", None, None)),
        check_vma=False,
    )
```
